32 devices in a mesh: seq: 8 (over y, x, core), mp: 4 (over z).
Axes of the slice: x: 2, y: 2, z: 4, core: 2. Of those that a mesh axis runs over, the one named last changes fastest.
Arguments:
- tokens: bfloat16 [1024, 4096], P('seq', 'mp'), may hold values from -10 to 10
- norm_gain: float32 [4096], replicated, may hold values from 0.1 to 1.9
- w_cand: bfloat16 [4096, 4096], P('seq', 'mp'), may hold values from -0.125 to 0.125
- w_gate: bfloat16 [4096, 4096], P('seq', 'mp'), may hold values from -0.046875 to 0.046875
- rec_gate: float32 [4096], P('mp'), may hold values from -0.75 to 0.75
- rec_cand: float32 [4096], P('mp'), may hold values from -0.6 to 0.6
- bias_gate: float32 [4096], P('mp')
- w_out: bfloat16 [4096, 4096], P('mp'), may hold values from -0.09375 to 0.09375
Outputs:
- output: bfloat16 [1024, 4096], P('seq', 'mp')
The draws below stay inside these ranges and needn't reach their ends.
All inputs are finite; a program needn't handle non-finite values.
Results may differ from the reference program's by a relative error of at most 0.0048.
Values may be sent and summed in bfloat16 or wider, within the bound.
A program may use at most 64 MiB of HBM per device.

```python
import jax
import jax.numpy as jnp
from jax import lax

D = 4096
NEWTON = 3
LENGTH = 1024


def draw_bias_gate(key, part):
    first = jax.random.fold_in(key, 0)
    lowest = jnp.log(0.3 / LENGTH)
    highest = jnp.log(0.03)
    lograte = jax.random.uniform(first, (D,), jnp.float32, lowest, highest)
    rate = jnp.exp(lograte)
    return jnp.log((1.0 - rate) / rate)


def draw_tokens(key, part):
    first, second = jax.random.split(jax.random.fold_in(key, 71), 2)
    segment = (jnp.arange(LENGTH) * 8 // LENGTH).astype(jnp.int32)
    topics = 2.0 * jnp.clip(jax.random.normal(first, (8, D), jnp.float32), -2.5, 2.5)
    noise = jnp.clip(jax.random.normal(second, (LENGTH, D), jnp.float32), -3.0, 3.0)
    values = jnp.take(topics, segment, axis=0) + noise
    return jnp.clip(values, -10.0, 10.0).astype(jnp.bfloat16)


def levels(own_key, shape, cuts, low, largest):
    def one(position, blocks):
        draws = jax.random.uniform(jax.random.fold_in(jax.random.fold_in(own_key, 6), position), (blocks,), jnp.float32, low / len(cuts), largest / len(cuts))
        return jnp.repeat(jnp.exp(draws), shape[position] // blocks).reshape((-1,) + (1,) * (len(shape) - position - 1))

    loudness = one(*cuts[0])
    for cut in cuts[1:]:
        loudness = loudness * one(*cut)
    return loudness


def scatter_about(key, dims, deviation, limit, pieces=(), kind=jnp.bfloat16):
    values = jax.random.normal(key, dims, jnp.float32) * deviation
    if len(pieces) > 0:
        values = levels(key, dims, pieces, -0.22, 0.18) * values
    return jnp.clip(values, min=-limit, max=limit).astype(kind)


def setup_inputs(seed: int = 0) -> dict:
    streams_of = jax.random.split(jax.random.key(seed), 9)
    return {
        "tokens": draw_tokens(jax.random.fold_in(streams_of[8], 71), 0),
        "norm_gain": jnp.clip(1.0 + 0.18 * jax.random.normal(streams_of[1], (D,), jnp.float32), 0.1, 1.9),
        "w_cand": scatter_about(streams_of[2], (D, D), (D // 2) ** -0.5, 0.125, ((0, 8), (1, 4))),
        "w_gate": scatter_about(streams_of[3], (D, D), (4 * D) ** -0.5, 0.046875, ((0, 8), (1, 4))),
        "rec_gate": jnp.clip(jax.random.uniform(streams_of[4], (D,), jnp.float32, -0.75, 0.75) * levels(streams_of[4], (D,), ((0, 4),), -0.4, 0.0), -0.75, 0.75),
        "rec_cand": jnp.clip(jax.random.uniform(streams_of[5], (D,), jnp.float32, -0.6, 0.6) * levels(streams_of[5], (D,), ((0, 4),), -0.4, 0.0), -0.6, 0.6),
        "bias_gate": draw_bias_gate(jax.random.fold_in(streams_of[8], 71), 0),
        "w_out": scatter_about(streams_of[7], (D, D), D ** -0.5, 0.09375, ((0, 4),)),
    }


def compose(earlier, later):
    return (later[0] * earlier[0], later[0] * earlier[1] + later[1])

def cell(previous, cand_pre, gate_pre, rec_gate, rec_cand, bias_gate):
    gate = jax.nn.sigmoid(gate_pre + rec_gate * previous + bias_gate)
    cand = jnp.tanh(cand_pre + rec_cand * previous)
    value = gate * previous + (1.0 - gate) * cand
    slope = gate + gate * (1.0 - gate) * rec_gate * (previous - cand) + (1.0 - gate) * (1.0 - cand * cand) * rec_cand
    return (value, slope)

def reference(tokens, norm_gain, w_cand, w_gate, rec_gate, rec_cand, bias_gate, w_out):
    wide = tokens.astype(jnp.float32)
    factor = lax.rsqrt(lax.optimization_barrier(jnp.mean(wide * wide, axis=1, keepdims=True)) + 1e-05)
    normed = (wide * factor * norm_gain).astype(jnp.bfloat16)
    cand_pre = jnp.dot(normed, w_cand, preferred_element_type=jnp.float32)
    gate_pre = jnp.dot(normed, w_gate, preferred_element_type=jnp.float32)
    state = jnp.zeros(cand_pre.shape, jnp.float32)
    for newton_step in range(NEWTON):
        previous = jnp.concatenate([jnp.zeros((1, state.shape[1]), jnp.float32), state[:-1]], axis=0)
        value, slope = cell(previous, cand_pre, gate_pre, rec_gate, rec_cand, bias_gate)
        offset = value - slope * previous
        sweep = lax.associative_scan(compose, (slope, offset), axis=0)
        state = sweep[1]
    state_b = state.astype(jnp.bfloat16)
    return jnp.dot(state_b, w_out, preferred_element_type=jnp.float32).astype(jnp.bfloat16)
```

```python
import functools

import jax
import jax.numpy as jnp
from jax import lax
from jax.experimental import pallas as pl
from jax.experimental.pallas import tpu as pltpu
from jax.sharding import PartitionSpec as P

NEWTON = 3


def prefix(value, axis, join, neutral):
    count, mine = (lax.axis_size(axis), lax.axis_index(axis))
    pieces = jax.tree.map(lambda part: lax.all_gather(part, axis), value)
    subtotal = jax.tree.map(
        lambda part, zero: jnp.full_like(part, 0) + jnp.asarray(zero, part.dtype), value, neutral
    )

    def lap(position, subtotal):
        longer = join(subtotal, jax.tree.map(lambda part: part[position], pieces))
        return jax.tree.map(lambda new, old: jnp.where(position < mine, new, old), longer, subtotal)

    return lax.fori_loop(0, count - 1, lap, subtotal)


def compose(earlier, later):
    return (later[0] * earlier[0], later[0] * earlier[1] + later[1])


def cell(previous, cand_pre, gate_pre, rec_gate, rec_cand, bias_gate):
    gate = jax.nn.sigmoid(gate_pre + rec_gate * previous + bias_gate)
    cand = jnp.tanh(cand_pre + rec_cand * previous)
    value = gate * previous + (1.0 - gate) * cand
    slope = (
        gate
        + gate * (1.0 - gate) * rec_gate * (previous - cand)
        + (1.0 - gate) * (1.0 - cand * cand) * rec_cand
    )
    return (value, slope)


def per_device(tokens, norm_gain, w_cand, w_gate, rec_gate, rec_cand, bias_gate, w_out):
    tok_rows = tokens.shape[0]
    channels = w_cand.shape[1]
    whole = lax.all_gather(tokens, "mp", axis=1, tiled=True)
    wide = whole.astype(jnp.float32)
    factor = lax.rsqrt(jnp.mean(wide * wide, axis=1, keepdims=True) + 1e-05)
    normed = (wide * factor * norm_gain).astype(jnp.bfloat16)
    cand_pre = jnp.dot(
        normed,
        lax.all_gather(w_cand, "seq", axis=0, tiled=True),
        preferred_element_type=jnp.float32,
    )
    gate_pre = jnp.dot(
        normed,
        lax.all_gather(w_gate, "seq", axis=0, tiled=True),
        preferred_element_type=jnp.float32,
    )
    state = jnp.zeros((tok_rows, channels), jnp.float32)
    carried = jnp.zeros((channels,), jnp.float32)
    ones_row = jnp.ones((channels,), jnp.float32)
    for newton_step in range(NEWTON):
        previous = jnp.concatenate([carried[None, :], state[:-1]], axis=0)
        value, slope = cell(previous, cand_pre, gate_pre, rec_gate, rec_cand, bias_gate)
        offset = value - slope * previous
        sweep_a, sweep_b = lax.associative_scan(compose, (slope, offset), axis=0)
        entering = prefix((sweep_a[-1], sweep_b[-1]), "seq", compose, (ones_row, carried * 0.0))
        carried = entering[1]
        state = sweep_a * carried + sweep_b
    state_b = state.astype(jnp.bfloat16)
    partial_sums = jnp.dot(state_b, w_out, preferred_element_type=jnp.float32)
    summed = lax.psum_scatter(partial_sums, "mp", scatter_dimension=1, tiled=True)
    return summed.astype(jnp.bfloat16)


def linear(first, previous, cand_pre, half_pre, half_gate, rec_gate, rec_cand):
    if first:
        gate = 0.5 * jnp.tanh(half_pre) + 0.5
        cand = jnp.tanh(cand_pre)
        apart = -cand
    else:
        gate = 0.5 * jnp.tanh(half_pre + half_gate * previous) + 0.5
        cand = jnp.tanh(cand_pre + rec_cand * previous)
        apart = previous - cand
    other = 1.0 - gate
    moved = gate * apart
    slope = gate + other * (rec_gate * moved + rec_cand * (1.0 - cand * cand))
    offset = cand + moved
    return slope, offset if first else offset - slope * previous


CORES = 2
SUBLANES = 8
LANES = 128
SIZES = (16,) * 8
PIECES = len(SIZES)
STARTS = tuple(sum(SIZES[:i]) for i in range(PIECES))
HALVES = 2
LAG = 2
LOOK = 2
WO_TURN = 8
UNROLL = 4
OWN = 1
BL = 1
CL = 2
ORDER = "cbd"
GROUP = 16
MESH = pl.DeviceIdType.MESH


def fused_kernel(
    n_seq,
    n_mp,
    tok_hbm,
    gain_ref,
    wc_hbm,
    wg_hbm,
    rg_ref,
    rc_ref,
    bg_ref,
    wo_hbm,
    out_ref,
    tok_ref,
    raw,
    xk,
    xn,
    sq_own,
    sq_all,
    f_own,
    f_all,
    f_col,
    wk,
    wo,
    own,
    onward,
    psend,
    precv,
    cand_n,
    gate_n,
    sweep_a,
    sweep_b,
    carry,
    ssend,
    sall,
    pout,
    osend,
    orecv,
    w_loc,
    w_snd,
    w_rcv,
    wo_sem,
    tok_sem,
    z_snd,
    z_rcv,
    k_snd,
    k_rcv,
    f_snd,
    q_snd,
    q_rcv,
    g_snd,
    g_rcv,
    p_snd,
    p_rcv,
    s_snd,
    s_rcv,
    o_snd,
    o_rcv,
):
    s, m = (lax.axis_index("seq"), lax.axis_index("mp"))
    n_chip = n_seq // CORES
    c, r = (s // CORES, s % CORES)
    mate = c * CORES + (1 - r)
    rows = tok_ref.shape[0]
    tokens = rows * n_seq
    k_own = wc_hbm.shape[0]
    width = raw.shape[2]
    q = r * n_chip + c

    def remote(src, dst, snd, rcv, **where):
        return pltpu.make_async_remote_copy(
            src_ref=src, dst_ref=dst, send_sem=snd, recv_sem=rcv, device_id=where, device_id_type=MESH
        )

    def greet():
        sem = pltpu.get_barrier_semaphore()
        for o in range(1, n_seq):
            pl.semaphore_signal(sem, inc=1, device_id={"seq": (s + o) % n_seq}, device_id_type=MESH)
        for o in range(1, n_mp):
            pl.semaphore_signal(sem, inc=1, device_id={"mp": (m + o) % n_mp}, device_id_type=MESH)

    def w_piece(hbm, core, chip):
        return hbm.at[:, pl.ds(pl.multiple_of((core * n_chip + chip) * LANES, LANES), LANES)]

    def w_place(i, chip, core):
        return wk.at[chip, pl.ds(pl.multiple_of(core * k_own, k_own), k_own), pl.ds(i * LANES, LANES)]

    local = [
        pltpu.make_async_copy(w_piece(hbm, r, chip), w_place(i, chip, r), w_loc)
        for chip in range(n_chip)
        for i, hbm in enumerate((wc_hbm, wg_hbm))
    ]
    wo_copy = pltpu.make_async_copy(wo_hbm, wo, wo_sem)
    greet()
    tok_copy = pltpu.make_async_copy(tok_hbm, tok_ref, tok_sem)
    tok_copy.start()
    for copy in local:
        copy.start()
    tok_copy.wait()
    across = lax.broadcasted_iota(jnp.int32, (rows, rows), 0) == lax.broadcasted_iota(
        jnp.int32, (rows, rows), 1
    )
    wide = tok_ref[...].astype(jnp.float32)
    squares = jnp.sum(wide * wide, axis=1, keepdims=True)
    squares = jnp.sum(jnp.where(across, squares, 0.0), axis=0, keepdims=True)
    sq_own[...] = jnp.broadcast_to(squares, sq_own.shape)
    pl.semaphore_wait(pltpu.get_barrier_semaphore(), n_seq + n_mp - 2)

    def piece(p):
        return pl.ds(STARTS[p], SIZES[p])

    def place(p, seq):
        return pl.ds(pl.multiple_of(STARTS[p] * n_seq + seq * SIZES[p], SUBLANES * 2), SIZES[p])

    def block(p):
        return pl.ds(STARTS[p] * n_seq, SIZES[p] * n_seq)

    def z_copy(src, b, p, d):
        return remote(src, raw.at[b, piece(p)], z_snd, z_rcv.at[b, p], mp=d)

    def relayed(b, d):
        return ((b == 1) & (d == 3)) | ((b == 2) & (d == 0))

    def plane_copy(src, b, p):
        seq = jnp.where(b == c, mate, b * CORES + r)
        lane_in = jnp.where(b == c, 1, 0)
        return remote(src, xk.at[place(p, s)], k_snd, k_rcv.at[lane_in, p], seq=seq)

    def z_send(p):
        for d in range(n_mp - 1, 0, -1):

            @pl.when((d > m) & jnp.logical_not(relayed(m, d)))
            def _():
                z_copy(tok_ref.at[piece(p)], m, p, d).start()

        for d in range(n_mp - 1):

            @pl.when((d < m) & jnp.logical_not(relayed(m, d)))
            def _():
                z_copy(tok_ref.at[piece(p)], m, p, d).start()

    def send_own(p):
        plane_copy(tok_ref.at[piece(p)], m, p).start()

        @pl.when(m == c)
        def _():
            xk[place(p, s), :] = tok_ref[piece(p), :]

    def pass_on(p, k):
        for sign in (-1, 1):
            b = m + sign * k

            @pl.when((b >= 0) & (b <= n_mp - 1))
            def _():
                here = raw.at[b, piece(p)]
                z_copy(here, b, p, m).wait_recv()
                if k == 1:
                    far = n_mp - 1 if sign < 0 else 0

                    @pl.when(m == (n_mp - 2 if sign < 0 else 1))
                    def _():
                        z_copy(here, b, p, far).start()

                plane_copy(here, b, p).start()

                @pl.when(b == c)
                def _():
                    xk[place(p, s), :] = raw[b, piece(p), :]

    for o in range(1, n_mp):
        copy = remote(sq_own, sq_all.at[o], q_snd, q_rcv, mp=(m + o) % n_mp)
        copy.start()
    for p in range(LOOK):
        z_send(p)
    for p in range(OWN):
        send_own(p)

    w_out_copies = [
        remote(w_piece(hbm, 1 - r, chip), w_place(i, chip, r), w_snd, w_rcv, seq=mate)
        for chip in range(n_chip)
        for i, hbm in enumerate((wc_hbm, wg_hbm))
    ]
    for copy in w_out_copies:
        copy.start()
    wide_rows = width // LANES
    gain = jnp.concatenate([gain_ref[pl.ds(c * wide_rows + i, 1), :] for i in range(wide_rows)], axis=1)
    bias = bg_ref[pl.ds(q, 1), :]
    half_gate = rg_ref[pl.ds(q, 1), :] * 0.5
    rec_gate = rg_ref[pl.ds(q, 1), :]
    rec_cand = rc_ref[pl.ds(q, 1), :]

    def stage_a(p):
        if p + LOOK < PIECES:
            z_send(p + LOOK)
        if p + OWN < PIECES:
            send_own(p + OWN)
        for k in range(1, n_mp):
            pass_on(p, k)
            if p == 0 and k == 1:
                factors()

    def factors():
        total = sq_own[...]
        others = sq_all.at[pl.ds(1, n_mp - 1)]
        remote(others, others, q_snd, q_rcv, mp=m).wait_recv()
        for o in range(1, n_mp):
            total = total + sq_all[o]
        f_own[...] = lax.rsqrt(total / (width * n_mp) + 1e-05)
        for o in range(1, n_seq):
            copy = remote(f_own, f_all.at[s], g_snd, g_rcv, seq=(s + o) % n_seq)
            copy.start()
        f_all[pl.ds(s, 1)] = f_own[...][None]

    def spread_factors():
        others = f_all.at[pl.ds(1, n_seq - 1)]
        remote(others, others, g_snd, g_rcv, seq=s).wait_recv()
        for i in range(n_seq):
            row = f_all[i, 0:1, :]
            column = jnp.sum(jnp.where(across, row, 0.0), axis=1, keepdims=True)
            column = jnp.broadcast_to(column, (rows, LANES))
            for start, size in zip(STARTS, SIZES):
                f_col[start * n_seq + i * size : start * n_seq + (i + 1) * size, :] = column[start : start + size, :]

    def arrived(p, lane_in):
        of = xk.at[pl.ds(0, (n_chip - 1 + lane_in) * SIZES[p])]
        remote(of, of, k_snd, k_rcv.at[lane_in, p], seq=s).wait_recv()

    def stage_b(p):
        arrived(p, 0)
        for o in range(1, n_chip):
            there = ((c + n_chip - o) % n_chip) * CORES + r
            copy = remote(
                xk.at[place(p, there)], xk.at[place(p, there)], f_snd, k_rcv.at[1, p], seq=mate
            )
            copy.start()

    def stage_c(p):
        arrived(p, 1)

        tile = SIZES[p] * n_seq

        @pl.loop(0, tile // GROUP, unroll=UNROLL)
        def _(i):
            at = pl.ds(pl.multiple_of(i * GROUP, GROUP), GROUP)
            of = pl.ds(pl.multiple_of(STARTS[p] * n_seq + i * GROUP, GROUP), GROUP)
            xn[at, :] = (xk[of, :].astype(jnp.float32) * f_col[of, 0:1] * gain).astype(jnp.bfloat16)

        def product(chip):
            return jnp.dot(xn[:tile, :], wk[chip], preferred_element_type=jnp.float32)

        at = block(p)
        first, second = ends(p)
        psend[1, at, :] = product(n_chip - 1 - c).astype(jnp.bfloat16)
        sums(1, p, first).start()
        psend[0, at, :] = product(first).astype(jnp.bfloat16)
        sums(0, p, first).start()
        onward[at, :] = product(second)
        own[at, :] = product(c)

    def ends(p):
        beside, above = (c + 1 - 2 * (c % 2), (c + n_chip // 2) % n_chip)
        return (beside, above) if p % 2 == 0 else (above, beside)

    def sums(slot, p, chip):
        at = block(p)
        return remote(
            psend.at[slot, at], precv.at[slot, at], p_snd, p_rcv.at[int(slot != 1), p], seq=chip * CORES + r
        )

    def stage_d(p):
        _, second = ends(p)
        sums(1, p, second).wait_recv()

        @pl.loop(0, SIZES[p] * n_seq // GROUP)
        def _(i):
            at = pl.ds(pl.multiple_of(STARTS[p] * n_seq + i * GROUP, GROUP), GROUP)
            psend[2, at, :] = (onward[at, :] + precv[1, at, :].astype(jnp.float32)).astype(jnp.bfloat16)

        sums(2, p, second).start()

    for turn in range(PIECES + CL + LAG):
        if turn < PIECES:
            stage_a(turn)
        if turn == CL - 1:
            spread_factors()
            part = wk.at[pl.ds(0, n_chip // 2)]
            pltpu.make_async_copy(part, part, w_loc).wait()
            remote(part, part, w_snd, w_rcv, seq=s).wait_recv()
        if turn == WO_TURN:
            wo_copy.start()
        for what in ORDER:
            if what == "c" and 0 <= turn - CL < PIECES:
                stage_c(turn - CL)
            if what == "b" and 0 <= turn - BL < PIECES:
                stage_b(turn - BL)
            if what == "d" and 0 <= turn - CL - LAG < PIECES:
                stage_d(turn - CL - LAG)

    def gather_piece(p):
        both = precv.at[pl.ds(0, 2), block(p)]
        remote(both, both, p_snd, p_rcv.at[1, p], seq=s).wait_recv()

        @pl.loop(0, SIZES[p] * n_seq // GROUP)
        def _(i):
            at = pl.ds(pl.multiple_of(STARTS[p] * n_seq + i * GROUP, GROUP), GROUP)
            value = own[at, :]
            for slot in (0, 2):
                value = value + precv[slot, at, :].astype(jnp.float32)
            cand_n[at, :] = value[:, :LANES]
            gate_n[at, :] = (value[:, LANES:] + bias) * 0.5

    for newton_step in range(NEWTON):
        zero = jnp.zeros((n_seq, LANES), jnp.float32)
        entering = zero if newton_step == 0 else carry[...]
        held = (entering, zero + 1.0, zero)
        for p in range(PIECES):
            if newton_step == 0:
                gather_piece(p)

            def lap(i, held):
                previous, a, b = held
                j = STARTS[p] + i
                at = pl.ds(STARTS[p] * n_seq + i, n_seq, stride=SIZES[p])
                slope, offset = linear(newton_step == 0, previous, cand_n[at, :], gate_n[at, :], half_gate, rec_gate, rec_cand)
                if newton_step > 0:
                    previous = sweep_a[j] * entering + sweep_b[j]
                a, b = (slope * a, slope * b + offset)
                sweep_a[j] = a
                sweep_b[j] = b
                return (previous, a, b)

            held = lax.fori_loop(0, SIZES[p], lap, held, unroll=8)
        _, a, b = held
        state = jnp.zeros((1, LANES), jnp.float32)
        for i in range(n_seq):
            carry[i : i + 1, :] = state
            state = a[i : i + 1, :] * state + b[i : i + 1, :]
    entering = carry[...]
    for p in range(PIECES):

        @pl.loop(0, SIZES[p], unroll=8)
        def _(i):
            j = STARTS[p] + i
            cand_n[pl.ds(STARTS[p] * n_seq + i, n_seq, stride=SIZES[p]), :] = sweep_a[j] * entering + sweep_b[j]

    for i in range(n_seq):
        for p in range(PIECES):
            start, size = STARTS[p] * n_seq + i * SIZES[p], SIZES[p]
            ssend[i, piece(p), :] = cand_n[start : start + size, :].astype(jnp.bfloat16)
    lane = pl.ds(pl.multiple_of(q * LANES, LANES), LANES)
    for o in range(1, n_seq):
        there = (s + o) % n_seq
        copy = remote(ssend.at[there], sall.at[:, lane], s_snd, s_rcv, seq=there)
        copy.start()
    sall[:, lane] = ssend[pl.ds(s, 1)].reshape(rows, LANES)
    def sent(ref, sem):
        remote(ref, ref, sem, s_rcv, seq=s).wait_send()

    sent(wk.at[pl.ds(0, n_chip // 2)], w_snd)
    sent(raw.at[pl.ds(0, n_mp - 1)], z_snd)
    sent(raw, k_snd)
    sent(raw.at[pl.ds(0, n_chip - 1)], f_snd)
    sent(sq_all.at[pl.ds(1, n_mp - 1)], q_snd)
    sent(f_all.at[pl.ds(1, n_seq - 1)], g_snd)
    sent(psend, p_snd)
    wo_copy.wait()
    others = ssend.at[pl.ds(1, n_seq - 1)]
    remote(others, others, s_snd, s_rcv, seq=s).wait_recv()

    cols = out_ref.shape[1]
    half = rows // HALVES

    def hop(side, d, h):
        there = (m + 1) % n_mp if side == 0 else (m + n_mp - 1) % n_mp
        at = pl.ds(h * half, half)
        return remote(
            osend.at[d, at], orecv.at[side, d, at], o_snd, o_rcv.at[side, d, h], mp=there
        )

    def project(d):
        lanes = pl.ds(pl.multiple_of(d * cols, cols), cols)
        pout[...] = jnp.dot(sall[...], wo[:, lanes], preferred_element_type=jnp.float32)

    def send_sum(side, k, when):
        d = m + k if side == 0 else m - k
        inside = (d <= n_mp - 1) if side == 0 else (d >= 0)
        first = (m == 0) if side == 0 else (m == n_mp - 1)

        @pl.when(inside & when)
        def _():
            project(d)
            for h in range(HALVES):
                at = pl.ds(h * half, half)

                @pl.when(first)
                def _():
                    osend[d, at, :] = pout[at, :].astype(jnp.bfloat16)

                @pl.when(jnp.logical_not(first))
                def _():
                    hop(side, d, h).wait_recv()
                    osend[d, at, :] = (pout[at, :] + orecv[side, d, at, :].astype(jnp.float32)).astype(
                        jnp.bfloat16
                    )

                hop(side, d, h).start()

    for k in range(n_mp - 1, 1, -1):
        for side in range(2):
            send_sum(side, k, True)
    low = m < n_mp // 2
    send_sum(1, 1, low)
    send_sum(0, 1, True)
    send_sum(1, 1, jnp.logical_not(low))

    project(m)
    for side in range(2):

        @pl.when(m > 0 if side == 0 else m < n_mp - 1)
        def _():
            for h in range(HALVES):
                at = pl.ds(h * half, half)
                hop(side, m, h).wait_recv()
                pout[at, :] = pout[at, :] + orecv[side, m, at, :].astype(jnp.float32)

    out_ref[...] = pout[...].astype(jnp.bfloat16)

    sent(ssend.at[pl.ds(1, n_seq - 1)], s_snd)
    sent(osend.at[pl.ds(1, n_mp - 1)], o_snd)


def fused(n_seq, n_mp, tokens, norm_gain, w_cand, w_gate, rec_gate, rec_cand, bias_gate, w_out):
    rows, width = tokens.shape
    k_own, channels = w_cand.shape
    n_chip = n_seq // CORES
    length = rows * n_seq
    bf16, f32 = (jnp.bfloat16, jnp.float32)
    vmem, dma = (pltpu.VMEM, pltpu.SemaphoreType.DMA)
    whole = pl.BlockSpec(memory_space=pltpu.VMEM)
    far = pl.BlockSpec(memory_space=pl.ANY)
    per_channel = [part.reshape(n_seq, LANES) for part in (rec_gate, rec_cand, bias_gate)]
    return pl.pallas_call(
        functools.partial(fused_kernel, n_seq, n_mp),
        out_shape=pltpu.VMEM((rows, width), bf16),
        in_specs=[far, whole, far, far, whole, whole, whole, far],
        out_specs=whole,
        scratch_shapes=[
            vmem((rows, width), bf16),
            vmem((n_mp, rows, width), bf16),
            vmem((length, width), bf16),
            vmem((length * max(SIZES) // sum(SIZES), width), bf16),
            vmem((n_seq, LANES), f32),
            vmem((n_mp, n_seq, LANES), f32),
            vmem((n_seq, LANES), f32),
            vmem((n_seq, n_seq, LANES), f32),
            vmem((length, LANES), f32),
            vmem((n_chip, k_own * CORES, 2 * LANES), bf16),
            vmem(w_out.shape, bf16),
            vmem((length, 2 * LANES), f32),
            vmem((length, 2 * LANES), f32),
            vmem((n_chip - 1, length, 2 * LANES), bf16),
            vmem((n_chip - 1, length, 2 * LANES), bf16),
            vmem((length, LANES), f32),
            vmem((length, LANES), f32),
            vmem((rows, n_seq, LANES), f32),
            vmem((rows, n_seq, LANES), f32),
            vmem((n_seq, LANES), f32),
            vmem((n_seq, rows, LANES), bf16),
            vmem((rows, channels), bf16),
            vmem((rows, width), f32),
            vmem((n_mp, rows, width), bf16),
            vmem((2, n_mp, rows, width), bf16),
            dma,
            dma,
            dma,
            dma,
            dma,
            dma,
            dma((n_mp, PIECES)),
            dma,
            dma((2, PIECES)),
            dma,
            dma,
            dma,
            dma,
            dma,
            dma,
            dma((2, PIECES)),
            dma,
            dma,
            dma,
            dma((2, n_mp, HALVES)),
        ],
        compiler_params=pltpu.CompilerParams(collective_id=0, has_side_effects=True),
    )(tokens, norm_gain.reshape(-1, LANES), w_cand, w_gate, *per_channel, w_out)


def layer(n_seq, n_mp, *args):
    tokens, w_cand = (args[0], args[2])
    fits = (
        n_seq == SUBLANES
        and n_seq == 4 * CORES
        and n_seq // CORES == n_mp
        and w_cand.shape[1] == n_seq * LANES
        and tokens.shape[0] == LANES
        and tokens.shape[1] % LANES == 0
    )
    return fused(n_seq, n_mp, *args) if fits else per_device(*args)


def solution(mesh):
    placed = (
        P("seq", "mp"),
        P(),
        P("seq", "mp"),
        P("seq", "mp"),
        P("mp"),
        P("mp"),
        P("mp"),
        P("mp", None),
    )
    return jax.shard_map(
        functools.partial(layer, mesh.shape["seq"], mesh.shape["mp"]), mesh=mesh, in_specs=placed, out_specs=P("seq", "mp"), check_vma=False
    )
```

```python
import functools

import jax
import jax.numpy as jnp
from jax import lax
from jax.experimental import pallas as pl
from jax.experimental.pallas import tpu as pltpu
from jax.sharding import PartitionSpec as P

NEWTON = 3


def prefix(value, axis, join, neutral):
    count, mine = (lax.axis_size(axis), lax.axis_index(axis))
    pieces = jax.tree.map(lambda part: lax.all_gather(part, axis), value)
    subtotal = jax.tree.map(
        lambda part, zero: jnp.full_like(part, 0) + jnp.asarray(zero, part.dtype), value, neutral
    )

    def lap(position, subtotal):
        longer = join(subtotal, jax.tree.map(lambda part: part[position], pieces))
        return jax.tree.map(lambda new, old: jnp.where(position < mine, new, old), longer, subtotal)

    return lax.fori_loop(0, count - 1, lap, subtotal)


def compose(earlier, later):
    return (later[0] * earlier[0], later[0] * earlier[1] + later[1])


def cell(previous, cand_pre, gate_pre, rec_gate, rec_cand, bias_gate):
    gate = jax.nn.sigmoid(gate_pre + rec_gate * previous + bias_gate)
    cand = jnp.tanh(cand_pre + rec_cand * previous)
    value = gate * previous + (1.0 - gate) * cand
    slope = (
        gate
        + gate * (1.0 - gate) * rec_gate * (previous - cand)
        + (1.0 - gate) * (1.0 - cand * cand) * rec_cand
    )
    return (value, slope)


def per_device(tokens, norm_gain, w_cand, w_gate, rec_gate, rec_cand, bias_gate, w_out):
    tok_rows = tokens.shape[0]
    channels = w_cand.shape[1]
    whole = lax.all_gather(tokens, "mp", axis=1, tiled=True)
    wide = whole.astype(jnp.float32)
    factor = lax.rsqrt(jnp.mean(wide * wide, axis=1, keepdims=True) + 1e-05)
    normed = (wide * factor * norm_gain).astype(jnp.bfloat16)
    cand_pre = jnp.dot(
        normed,
        lax.all_gather(w_cand, "seq", axis=0, tiled=True),
        preferred_element_type=jnp.float32,
    )
    gate_pre = jnp.dot(
        normed,
        lax.all_gather(w_gate, "seq", axis=0, tiled=True),
        preferred_element_type=jnp.float32,
    )
    state = jnp.zeros((tok_rows, channels), jnp.float32)
    carried = jnp.zeros((channels,), jnp.float32)
    ones_row = jnp.ones((channels,), jnp.float32)
    for newton_step in range(NEWTON):
        previous = jnp.concatenate([carried[None, :], state[:-1]], axis=0)
        value, slope = cell(previous, cand_pre, gate_pre, rec_gate, rec_cand, bias_gate)
        offset = value - slope * previous
        sweep_a, sweep_b = lax.associative_scan(compose, (slope, offset), axis=0)
        entering = prefix((sweep_a[-1], sweep_b[-1]), "seq", compose, (ones_row, carried * 0.0))
        carried = entering[1]
        state = sweep_a * carried + sweep_b
    state_b = state.astype(jnp.bfloat16)
    partial_sums = jnp.dot(state_b, w_out, preferred_element_type=jnp.float32)
    summed = lax.psum_scatter(partial_sums, "mp", scatter_dimension=1, tiled=True)
    return summed.astype(jnp.bfloat16)


def linear(first, previous, cand_pre, half_pre, half_gate, rec_gate, rec_cand):
    if first:
        gate = 0.5 * jnp.tanh(half_pre) + 0.5
        cand = jnp.tanh(cand_pre)
        apart = -cand
    else:
        gate = 0.5 * jnp.tanh(half_pre + half_gate * previous) + 0.5
        cand = jnp.tanh(cand_pre + rec_cand * previous)
        apart = previous - cand
    other = 1.0 - gate
    moved = gate * apart
    slope = gate + other * (rec_gate * moved + rec_cand * (1.0 - cand * cand))
    offset = cand + moved
    return slope, offset if first else offset - slope * previous


CORES = 2
SUBLANES = 8
LANES = 128
SIZES = (16, 16, 32, 32, 32)
PIECES = len(SIZES)
STARTS = tuple(sum(SIZES[:i]) for i in range(PIECES))
HALVES = 2
RELAY = 1
NEAR = 1
FACTORS_AT = (0, 2)
LAG = 2
LOOK = 2
WO_TURN = 5
UNROLL = 4
OWN = 1
BL = 1
CL = 2
ORDER = "acbd"
GROUP = 16
MESH = pl.DeviceIdType.MESH


def fused_kernel(
    n_seq,
    n_mp,
    tok_hbm,
    gain_hbm,
    wc_hbm,
    wg_hbm,
    rg_hbm,
    rc_hbm,
    bg_hbm,
    wo_hbm,
    out_ref,
    tok_ref,
    gain_ref,
    rg_ref,
    rc_ref,
    bg_ref,
    raw,
    xk,
    xn,
    sq_own,
    sq_all,
    f_own,
    f_all,
    f_col,
    wk,
    wo,
    own,
    onward,
    psend,
    precv,
    cand_n,
    gate_n,
    sweep_a,
    sweep_b,
    carry,
    ssend,
    sall,
    pout,
    osend,
    orecv,
    w_loc,
    w_snd,
    w_rcv,
    wo_sem,
    tok_sem,
    small_sem,
    z_snd,
    z_rcv,
    k_snd,
    k_rcv,
    f_snd,
    q_snd,
    q_rcv,
    g_snd,
    g_rcv,
    p_snd,
    p_rcv,
    s_snd,
    s_rcv,
    o_snd,
    o_rcv,
):
    s, m = (lax.axis_index("seq"), lax.axis_index("mp"))
    n_chip = n_seq // CORES
    c, r = (s // CORES, s % CORES)
    mate = c * CORES + (1 - r)
    rows = tok_ref.shape[0]
    tokens = rows * n_seq
    k_own = wc_hbm.shape[0]
    width = raw.shape[2]
    q = r * n_chip + c

    def remote(src, dst, snd, rcv, **where):
        return pltpu.make_async_remote_copy(
            src_ref=src, dst_ref=dst, send_sem=snd, recv_sem=rcv, device_id=where, device_id_type=MESH
        )

    def greet():
        sem = pltpu.get_barrier_semaphore()
        for o in range(1, n_seq):
            pl.semaphore_signal(sem, inc=1, device_id={"seq": (s + o) % n_seq}, device_id_type=MESH)
        for o in range(1, n_mp):
            pl.semaphore_signal(sem, inc=1, device_id={"mp": (m + o) % n_mp}, device_id_type=MESH)

    def w_piece(hbm, core, chip):
        return hbm.at[:, pl.ds(pl.multiple_of((core * n_chip + chip) * LANES, LANES), LANES)]

    def w_place(i, chip, core):
        return wk.at[chip, pl.ds(pl.multiple_of(core * k_own, k_own), k_own), pl.ds(i * LANES, LANES)]

    local = [
        pltpu.make_async_copy(w_piece(hbm, r, chip), w_place(i, chip, r), w_loc)
        for chip in range(n_chip)
        for i, hbm in enumerate((wc_hbm, wg_hbm))
    ]
    wo_copy = pltpu.make_async_copy(wo_hbm, wo, wo_sem)
    greet()
    tok_copy = pltpu.make_async_copy(tok_hbm, tok_ref, tok_sem)
    tok_copy.start()
    for copy in local:
        copy.start()
    small = [
        pltpu.make_async_copy(src, dst, small_sem.at[i])
        for i, (src, dst) in enumerate(
            ((gain_hbm, gain_ref), (rg_hbm, rg_ref), (rc_hbm, rc_ref), (bg_hbm, bg_ref))
        )
    ]
    for copy in small:
        copy.start()
    pl.semaphore_wait(pltpu.get_barrier_semaphore(), n_seq + n_mp - 2)
    tok_copy.wait()

    def piece(p):
        return pl.ds(STARTS[p], SIZES[p])

    def place(p, seq):
        return pl.ds(pl.multiple_of(STARTS[p] * n_seq + seq * SIZES[p], SUBLANES * 2), SIZES[p])

    def block(p):
        return pl.ds(STARTS[p] * n_seq, SIZES[p] * n_seq)

    def z_copy(src, b, p, d):
        return remote(src, raw.at[b, piece(p)], z_snd, z_rcv.at[b, p], mp=d)

    def relayed(b, d):
        return (((b == 1) & (d == 3)) | ((b == 2) & (d == 0))) & (RELAY == 1)

    def plane_copy(src, b, p):
        seq = jnp.where(b == c, mate, b * CORES + r)
        lane_in = jnp.where(b == c, 1, 0)
        return remote(src, xk.at[place(p, s)], k_snd, k_rcv.at[lane_in, p], seq=seq)

    def z_send(p):
        ups, downs = (range(n_mp - 1, 0, -1), range(n_mp - 1))
        if NEAR:
            ups, downs = (ups[::-1], downs[::-1])
        for side, order in ((1, ups), (-1, downs)):
            for d in order:

                @pl.when(((d > m) if side > 0 else (d < m)) & jnp.logical_not(relayed(m, d)))
                def _():
                    z_copy(tok_ref.at[piece(p)], m, p, d).start()

    def send_own(p):
        plane_copy(tok_ref.at[piece(p)], m, p).start()

        @pl.when(m == c)
        def _():
            xk[place(p, s), :] = tok_ref[piece(p), :]

    def pass_on(p, k):
        low = m < n_mp // 2
        take(p, k, 1, low)
        take(p, k, -1, True)
        take(p, k, 1, jnp.logical_not(low))

    def take(p, k, sign, when):
        b = m + sign * k

        @pl.when((b >= 0) & (b <= n_mp - 1) & when)
        def _():
            here = raw.at[b, piece(p)]
            z_copy(here, b, p, m).wait_recv()
            if k == 1 and RELAY:
                far = n_mp - 1 if sign < 0 else 0

                @pl.when(m == (n_mp - 2 if sign < 0 else 1))
                def _():
                    z_copy(here, b, p, far).start()

            plane_copy(here, b, p).start()

            @pl.when(b == c)
            def _():
                xk[place(p, s), :] = raw[b, piece(p), :]

    z_send(0)
    send_own(0)
    across = lax.broadcasted_iota(jnp.int32, (rows, rows), 0) == lax.broadcasted_iota(
        jnp.int32, (rows, rows), 1
    )
    wide = tok_ref[...].astype(jnp.float32)
    squares = jnp.sum(wide * wide, axis=1, keepdims=True)
    squares = jnp.sum(jnp.where(across, squares, 0.0), axis=0, keepdims=True)
    sq_own[...] = jnp.broadcast_to(squares, sq_own.shape)
    for o in range(1, n_mp):
        remote(sq_own, sq_all.at[o], q_snd, q_rcv, mp=(m + o) % n_mp).start()
    for p in range(1, LOOK):
        z_send(p)
    for p in range(1, OWN):
        send_own(p)

    w_out_copies = [
        remote(w_piece(hbm, 1 - r, chip), w_place(i, chip, r), w_snd, w_rcv, seq=mate)
        for chip in range(n_chip)
        for i, hbm in enumerate((wc_hbm, wg_hbm))
    ]
    for copy in w_out_copies:
        copy.start()
    for copy in small:
        copy.wait()
    wide_rows = width // LANES
    gain = jnp.concatenate([gain_ref[pl.ds(c * wide_rows + i, 1), :] for i in range(wide_rows)], axis=1)
    bias = bg_ref[pl.ds(q, 1), :]
    half_gate = rg_ref[pl.ds(q, 1), :] * 0.5
    rec_gate = rg_ref[pl.ds(q, 1), :]
    rec_cand = rc_ref[pl.ds(q, 1), :]

    def stage_a(p):
        if p + LOOK < PIECES:
            z_send(p + LOOK)
        if p + OWN < PIECES:
            send_own(p + OWN)
        for k in range(1, n_mp):
            pass_on(p, k)
            if (p, k) == FACTORS_AT:
                factors()

    def factors():
        total = sq_own[...]
        others = sq_all.at[pl.ds(1, n_mp - 1)]
        remote(others, others, q_snd, q_rcv, mp=m).wait_recv()
        for o in range(1, n_mp):
            total = total + sq_all[o]
        f_own[...] = lax.rsqrt(total / (width * n_mp) + 1e-05)
        for o in range(1, n_seq):
            copy = remote(f_own, f_all.at[s], g_snd, g_rcv, seq=(s + o) % n_seq)
            copy.start()
        f_all[pl.ds(s, 1)] = f_own[...][None]

    def spread_factors():
        others = f_all.at[pl.ds(1, n_seq - 1)]
        remote(others, others, g_snd, g_rcv, seq=s).wait_recv()
        for i in range(n_seq):
            row = f_all[i, 0:1, :]
            column = jnp.sum(jnp.where(across, row, 0.0), axis=1, keepdims=True)
            column = jnp.broadcast_to(column, (rows, LANES))
            for start, size in zip(STARTS, SIZES):
                f_col[start * n_seq + i * size : start * n_seq + (i + 1) * size, :] = column[start : start + size, :]

    def arrived(p, lane_in):
        of = xk.at[pl.ds(0, (n_chip - 1 + lane_in) * SIZES[p])]
        remote(of, of, k_snd, k_rcv.at[lane_in, p], seq=s).wait_recv()

    def stage_b(p):
        arrived(p, 0)
        for o in range(1, n_chip):
            there = ((c + n_chip - o) % n_chip) * CORES + r
            copy = remote(
                xk.at[place(p, there)], xk.at[place(p, there)], f_snd, k_rcv.at[1, p], seq=mate
            )
            copy.start()

    def stage_c(p):
        arrived(p, 1)

        tile = SIZES[p] * n_seq

        @pl.loop(0, tile // GROUP, unroll=UNROLL)
        def _(i):
            at = pl.ds(pl.multiple_of(i * GROUP, GROUP), GROUP)
            of = pl.ds(pl.multiple_of(STARTS[p] * n_seq + i * GROUP, GROUP), GROUP)
            xn[at, :] = (xk[of, :].astype(jnp.float32) * f_col[of, 0:1] * gain).astype(jnp.bfloat16)

        def product(chip):
            return jnp.dot(xn[:tile, :], wk[chip], preferred_element_type=jnp.float32)

        at = block(p)
        first, second = ends(p)
        psend[1, at, :] = product(n_chip - 1 - c).astype(jnp.bfloat16)
        sums(1, p, first).start()
        psend[0, at, :] = product(first).astype(jnp.bfloat16)
        sums(0, p, first).start()
        onward[at, :] = product(second)
        own[at, :] = product(c)

    def ends(p):
        beside, above = (c + 1 - 2 * (c % 2), (c + n_chip // 2) % n_chip)
        return (beside, above) if p % 2 == 0 else (above, beside)

    def sums(slot, p, chip):
        at = block(p)
        return remote(
            psend.at[slot, at], precv.at[slot, at], p_snd, p_rcv.at[int(slot != 1), p], seq=chip * CORES + r
        )

    def stage_d(p):
        _, second = ends(p)
        sums(1, p, second).wait_recv()

        @pl.loop(0, SIZES[p] * n_seq // GROUP)
        def _(i):
            at = pl.ds(pl.multiple_of(STARTS[p] * n_seq + i * GROUP, GROUP), GROUP)
            psend[2, at, :] = (onward[at, :] + precv[1, at, :].astype(jnp.float32)).astype(jnp.bfloat16)

        sums(2, p, second).start()

    for turn in range(PIECES + CL + LAG):
        if turn == WO_TURN:
            wo_copy.start()
        for what in ORDER:
            if what == "a" and turn < PIECES:
                stage_a(turn)
            if what == "c" and 0 <= turn - CL < PIECES:
                if turn == CL:
                    spread_factors()
                    part = wk.at[pl.ds(0, n_chip // 2)]
                    pltpu.make_async_copy(part, part, w_loc).wait()
                    remote(part, part, w_snd, w_rcv, seq=s).wait_recv()
                stage_c(turn - CL)
            if what == "b" and 0 <= turn - BL < PIECES:
                stage_b(turn - BL)
            if what == "d" and 0 <= turn - CL - LAG < PIECES:
                stage_d(turn - CL - LAG)

    def gather_piece(p):
        both = precv.at[pl.ds(0, 2), block(p)]
        remote(both, both, p_snd, p_rcv.at[1, p], seq=s).wait_recv()

        @pl.loop(0, SIZES[p] * n_seq // GROUP)
        def _(i):
            at = pl.ds(pl.multiple_of(STARTS[p] * n_seq + i * GROUP, GROUP), GROUP)
            value = own[at, :]
            for slot in (0, 2):
                value = value + precv[slot, at, :].astype(jnp.float32)
            cand_n[at, :] = value[:, :LANES]
            gate_n[at, :] = (value[:, LANES:] + bias) * 0.5

    for newton_step in range(NEWTON):
        zero = jnp.zeros((n_seq, LANES), jnp.float32)
        entering = zero if newton_step == 0 else carry[...]
        held = (entering, zero + 1.0, zero)
        for p in range(PIECES):
            if newton_step == 0:
                gather_piece(p)

            def lap(i, held):
                previous, a, b = held
                j = STARTS[p] + i
                at = pl.ds(STARTS[p] * n_seq + i, n_seq, stride=SIZES[p])
                slope, offset = linear(newton_step == 0, previous, cand_n[at, :], gate_n[at, :], half_gate, rec_gate, rec_cand)
                if newton_step > 0:
                    previous = sweep_a[j] * entering + sweep_b[j]
                a, b = (slope * a, slope * b + offset)
                sweep_a[j] = a
                sweep_b[j] = b
                return (previous, a, b)

            held = lax.fori_loop(0, SIZES[p], lap, held, unroll=8)
        _, a, b = held
        state = jnp.zeros((1, LANES), jnp.float32)
        for i in range(n_seq):
            carry[i : i + 1, :] = state
            state = a[i : i + 1, :] * state + b[i : i + 1, :]
    entering = carry[...]
    for p in range(PIECES):

        @pl.loop(0, SIZES[p], unroll=8)
        def _(i):
            j = STARTS[p] + i
            cand_n[pl.ds(STARTS[p] * n_seq + i, n_seq, stride=SIZES[p]), :] = sweep_a[j] * entering + sweep_b[j]

    for i in range(n_seq):
        for p in range(PIECES):
            start, size = STARTS[p] * n_seq + i * SIZES[p], SIZES[p]
            ssend[i, piece(p), :] = cand_n[start : start + size, :].astype(jnp.bfloat16)
    lane = pl.ds(pl.multiple_of(q * LANES, LANES), LANES)
    for o in range(1, n_seq):
        there = (s + o) % n_seq
        copy = remote(ssend.at[there], sall.at[:, lane], s_snd, s_rcv, seq=there)
        copy.start()
    sall[:, lane] = ssend[pl.ds(s, 1)].reshape(rows, LANES)
    def sent(ref, sem):
        remote(ref, ref, sem, s_rcv, seq=s).wait_send()

    sent(wk.at[pl.ds(0, n_chip // 2)], w_snd)
    sent(raw.at[pl.ds(0, n_mp - 1)], z_snd)
    sent(raw, k_snd)
    sent(raw.at[pl.ds(0, n_chip - 1)], f_snd)
    sent(sq_all.at[pl.ds(1, n_mp - 1)], q_snd)
    sent(f_all.at[pl.ds(1, n_seq - 1)], g_snd)
    sent(psend, p_snd)
    wo_copy.wait()
    others = ssend.at[pl.ds(1, n_seq - 1)]
    remote(others, others, s_snd, s_rcv, seq=s).wait_recv()

    cols = out_ref.shape[1]
    half = rows // HALVES

    def hop(side, d, h):
        there = (m + 1) % n_mp if side == 0 else (m + n_mp - 1) % n_mp
        at = pl.ds(h * half, half)
        return remote(
            osend.at[d, at], orecv.at[side, d, at], o_snd, o_rcv.at[side, d, h], mp=there
        )

    def project(d):
        lanes = pl.ds(pl.multiple_of(d * cols, cols), cols)
        pout[...] = jnp.dot(sall[...], wo[:, lanes], preferred_element_type=jnp.float32)

    def send_sum(side, k, when):
        d = m + k if side == 0 else m - k
        inside = (d <= n_mp - 1) if side == 0 else (d >= 0)
        first = (m == 0) if side == 0 else (m == n_mp - 1)

        @pl.when(inside & when)
        def _():
            project(d)
            for h in range(HALVES):
                at = pl.ds(h * half, half)

                @pl.when(first)
                def _():
                    osend[d, at, :] = pout[at, :].astype(jnp.bfloat16)

                @pl.when(jnp.logical_not(first))
                def _():
                    hop(side, d, h).wait_recv()
                    osend[d, at, :] = (pout[at, :] + orecv[side, d, at, :].astype(jnp.float32)).astype(
                        jnp.bfloat16
                    )

                hop(side, d, h).start()

    for k in range(n_mp - 1, 1, -1):
        for side in range(2):
            send_sum(side, k, True)
    low = m < n_mp // 2
    send_sum(1, 1, low)
    send_sum(0, 1, True)
    send_sum(1, 1, jnp.logical_not(low))

    project(m)
    for side in range(2):

        @pl.when(m > 0 if side == 0 else m < n_mp - 1)
        def _():
            for h in range(HALVES):
                at = pl.ds(h * half, half)
                hop(side, m, h).wait_recv()
                pout[at, :] = pout[at, :] + orecv[side, m, at, :].astype(jnp.float32)

    out_ref[...] = pout[...].astype(jnp.bfloat16)

    sent(ssend.at[pl.ds(1, n_seq - 1)], s_snd)
    sent(osend.at[pl.ds(1, n_mp - 1)], o_snd)


def fused(n_seq, n_mp, tokens, norm_gain, w_cand, w_gate, rec_gate, rec_cand, bias_gate, w_out):
    rows, width = tokens.shape
    k_own, channels = w_cand.shape
    n_chip = n_seq // CORES
    length = rows * n_seq
    bf16, f32 = (jnp.bfloat16, jnp.float32)
    vmem, dma = (pltpu.VMEM, pltpu.SemaphoreType.DMA)
    whole = pl.BlockSpec(memory_space=pltpu.VMEM)
    far = pl.BlockSpec(memory_space=pl.ANY)
    per_channel = [part.reshape(n_seq, LANES) for part in (rec_gate, rec_cand, bias_gate)]
    return pl.pallas_call(
        functools.partial(fused_kernel, n_seq, n_mp),
        out_shape=pltpu.VMEM((rows, width), bf16),
        in_specs=[far] * 8,
        out_specs=whole,
        scratch_shapes=[
            vmem((rows, width), bf16),
            vmem((n_mp * width // LANES, LANES), f32),
            vmem((n_seq, LANES), f32),
            vmem((n_seq, LANES), f32),
            vmem((n_seq, LANES), f32),
            vmem((n_mp, rows, width), bf16),
            vmem((length, width), bf16),
            vmem((length * max(SIZES) // sum(SIZES), width), bf16),
            vmem((n_seq, LANES), f32),
            vmem((n_mp, n_seq, LANES), f32),
            vmem((n_seq, LANES), f32),
            vmem((n_seq, n_seq, LANES), f32),
            vmem((length, LANES), f32),
            vmem((n_chip, k_own * CORES, 2 * LANES), bf16),
            vmem(w_out.shape, bf16),
            vmem((length, 2 * LANES), f32),
            vmem((length, 2 * LANES), f32),
            vmem((n_chip - 1, length, 2 * LANES), bf16),
            vmem((n_chip - 1, length, 2 * LANES), bf16),
            vmem((length, LANES), f32),
            vmem((length, LANES), f32),
            vmem((rows, n_seq, LANES), f32),
            vmem((rows, n_seq, LANES), f32),
            vmem((n_seq, LANES), f32),
            vmem((n_seq, rows, LANES), bf16),
            vmem((rows, channels), bf16),
            vmem((rows, width), f32),
            vmem((n_mp, rows, width), bf16),
            vmem((2, n_mp, rows, width), bf16),
            dma,
            dma,
            dma,
            dma,
            dma,
            dma((4,)),
            dma,
            dma((n_mp, PIECES)),
            dma,
            dma((2, PIECES)),
            dma,
            dma,
            dma,
            dma,
            dma,
            dma,
            dma((2, PIECES)),
            dma,
            dma,
            dma,
            dma((2, n_mp, HALVES)),
        ],
        compiler_params=pltpu.CompilerParams(collective_id=0, has_side_effects=True),
    )(tokens, norm_gain.reshape(-1, LANES), w_cand, w_gate, *per_channel, w_out)


def layer(n_seq, n_mp, *args):
    tokens, w_cand = (args[0], args[2])
    fits = (
        n_seq == SUBLANES
        and n_seq == 4 * CORES
        and n_seq // CORES == n_mp
        and w_cand.shape[1] == n_seq * LANES
        and tokens.shape[0] == LANES
        and tokens.shape[1] % LANES == 0
    )
    return fused(n_seq, n_mp, *args) if fits else per_device(*args)


def solution(mesh):
    placed = (
        P("seq", "mp"),
        P(),
        P("seq", "mp"),
        P("seq", "mp"),
        P("mp"),
        P("mp"),
        P("mp"),
        P("mp", None),
    )
    return jax.shard_map(
        functools.partial(layer, mesh.shape["seq"], mesh.shape["mp"]), mesh=mesh, in_specs=placed, out_specs=P("seq", "mp"), check_vma=False
    )
```

```python
import functools

import jax
import jax.numpy as jnp
from jax import lax
from jax.experimental import pallas as pl
from jax.experimental.pallas import tpu as pltpu
from jax.sharding import PartitionSpec as P

NEWTON = 3


def prefix(value, axis, join, neutral):
    count, mine = (lax.axis_size(axis), lax.axis_index(axis))
    pieces = jax.tree.map(lambda part: lax.all_gather(part, axis), value)
    subtotal = jax.tree.map(
        lambda part, zero: jnp.full_like(part, 0) + jnp.asarray(zero, part.dtype), value, neutral
    )

    def lap(position, subtotal):
        longer = join(subtotal, jax.tree.map(lambda part: part[position], pieces))
        return jax.tree.map(lambda new, old: jnp.where(position < mine, new, old), longer, subtotal)

    return lax.fori_loop(0, count - 1, lap, subtotal)


def compose(earlier, later):
    return (later[0] * earlier[0], later[0] * earlier[1] + later[1])


def cell(previous, cand_pre, gate_pre, rec_gate, rec_cand, bias_gate):
    gate = jax.nn.sigmoid(gate_pre + rec_gate * previous + bias_gate)
    cand = jnp.tanh(cand_pre + rec_cand * previous)
    value = gate * previous + (1.0 - gate) * cand
    slope = (
        gate
        + gate * (1.0 - gate) * rec_gate * (previous - cand)
        + (1.0 - gate) * (1.0 - cand * cand) * rec_cand
    )
    return (value, slope)


def per_device(tokens, norm_gain, w_cand, w_gate, rec_gate, rec_cand, bias_gate, w_out):
    tok_rows = tokens.shape[0]
    channels = w_cand.shape[1]
    whole = lax.all_gather(tokens, "mp", axis=1, tiled=True)
    wide = whole.astype(jnp.float32)
    factor = lax.rsqrt(jnp.mean(wide * wide, axis=1, keepdims=True) + 1e-05)
    normed = (wide * factor * norm_gain).astype(jnp.bfloat16)
    cand_pre = jnp.dot(
        normed,
        lax.all_gather(w_cand, "seq", axis=0, tiled=True),
        preferred_element_type=jnp.float32,
    )
    gate_pre = jnp.dot(
        normed,
        lax.all_gather(w_gate, "seq", axis=0, tiled=True),
        preferred_element_type=jnp.float32,
    )
    state = jnp.zeros((tok_rows, channels), jnp.float32)
    carried = jnp.zeros((channels,), jnp.float32)
    ones_row = jnp.ones((channels,), jnp.float32)
    for newton_step in range(NEWTON):
        previous = jnp.concatenate([carried[None, :], state[:-1]], axis=0)
        value, slope = cell(previous, cand_pre, gate_pre, rec_gate, rec_cand, bias_gate)
        offset = value - slope * previous
        sweep_a, sweep_b = lax.associative_scan(compose, (slope, offset), axis=0)
        entering = prefix((sweep_a[-1], sweep_b[-1]), "seq", compose, (ones_row, carried * 0.0))
        carried = entering[1]
        state = sweep_a * carried + sweep_b
    state_b = state.astype(jnp.bfloat16)
    partial_sums = jnp.dot(state_b, w_out, preferred_element_type=jnp.float32)
    summed = lax.psum_scatter(partial_sums, "mp", scatter_dimension=1, tiled=True)
    return summed.astype(jnp.bfloat16)


def linear(first, previous, cand_pre, half_pre, half_gate, rec_gate, rec_cand):
    if first:
        gate = 0.5 * jnp.tanh(half_pre) + 0.5
        cand = jnp.tanh(cand_pre)
        apart = -cand
    else:
        gate = 0.5 * jnp.tanh(half_pre + half_gate * previous) + 0.5
        cand = jnp.tanh(cand_pre + rec_cand * previous)
        apart = previous - cand
    other = 1.0 - gate
    moved = gate * apart
    slope = gate + other * (rec_gate * moved + rec_cand * (1.0 - cand * cand))
    offset = cand + moved
    return slope, offset if first else offset - slope * previous


CORES = 2
SUBLANES = 8
LANES = 128
SIZES = (16, 16, 32, 32, 16, 16)
PIECES = len(SIZES)
STARTS = tuple(sum(SIZES[:i]) for i in range(PIECES))
HALVES = 2
RELAY = 1
NEAR = 1
FACTORS_AT = (0, 2)
LAG = 2
LOOK = 2
WO_TURN = 6
UNROLL = 4
OWN = 1
BL = 1
CL = 2
ORDER = "acbd"
GROUP = 16
MESH = pl.DeviceIdType.MESH


def fused_kernel(
    n_seq,
    n_mp,
    tok_hbm,
    gain_hbm,
    wc_hbm,
    wg_hbm,
    rg_hbm,
    rc_hbm,
    bg_hbm,
    wo_hbm,
    out_ref,
    tok_ref,
    gain_ref,
    rg_ref,
    rc_ref,
    bg_ref,
    raw,
    xk,
    xn,
    sq_own,
    sq_all,
    f_own,
    f_all,
    f_col,
    wk,
    wo,
    own,
    onward,
    psend,
    precv,
    cand_n,
    gate_n,
    sweep_a,
    sweep_b,
    carry,
    ssend,
    sall,
    pout,
    osend,
    orecv,
    w_loc,
    w_snd,
    w_rcv,
    wo_sem,
    tok_sem,
    small_sem,
    z_snd,
    z_rcv,
    k_snd,
    k_rcv,
    f_snd,
    q_snd,
    q_rcv,
    g_snd,
    g_rcv,
    p_snd,
    p_rcv,
    s_snd,
    s_rcv,
    o_snd,
    o_rcv,
):
    s, m = (lax.axis_index("seq"), lax.axis_index("mp"))
    n_chip = n_seq // CORES
    c, r = (s // CORES, s % CORES)
    mate = c * CORES + (1 - r)
    rows = tok_ref.shape[0]
    tokens = rows * n_seq
    k_own = wc_hbm.shape[0]
    width = raw.shape[2]
    q = r * n_chip + c

    def remote(src, dst, snd, rcv, **where):
        return pltpu.make_async_remote_copy(
            src_ref=src, dst_ref=dst, send_sem=snd, recv_sem=rcv, device_id=where, device_id_type=MESH
        )

    def greet():
        sem = pltpu.get_barrier_semaphore()
        for o in range(1, n_seq):
            pl.semaphore_signal(sem, inc=1, device_id={"seq": (s + o) % n_seq}, device_id_type=MESH)
        for o in range(1, n_mp):
            pl.semaphore_signal(sem, inc=1, device_id={"mp": (m + o) % n_mp}, device_id_type=MESH)

    def w_piece(hbm, core, chip):
        return hbm.at[:, pl.ds(pl.multiple_of((core * n_chip + chip) * LANES, LANES), LANES)]

    def w_place(i, chip, core):
        return wk.at[chip, pl.ds(pl.multiple_of(core * k_own, k_own), k_own), pl.ds(i * LANES, LANES)]

    local = [
        pltpu.make_async_copy(w_piece(hbm, r, chip), w_place(i, chip, r), w_loc)
        for chip in range(n_chip)
        for i, hbm in enumerate((wc_hbm, wg_hbm))
    ]
    wo_copy = pltpu.make_async_copy(wo_hbm, wo, wo_sem)
    greet()
    tok_copy = pltpu.make_async_copy(tok_hbm, tok_ref, tok_sem)
    tok_copy.start()
    for copy in local:
        copy.start()
    small = [
        pltpu.make_async_copy(src, dst, small_sem.at[i])
        for i, (src, dst) in enumerate(
            ((gain_hbm, gain_ref), (rg_hbm, rg_ref), (rc_hbm, rc_ref), (bg_hbm, bg_ref))
        )
    ]
    for copy in small:
        copy.start()
    pl.semaphore_wait(pltpu.get_barrier_semaphore(), n_seq + n_mp - 2)
    tok_copy.wait()

    def piece(p):
        return pl.ds(STARTS[p], SIZES[p])

    def place(p, seq):
        return pl.ds(pl.multiple_of(STARTS[p] * n_seq + seq * SIZES[p], SUBLANES * 2), SIZES[p])

    def block(p):
        return pl.ds(STARTS[p] * n_seq, SIZES[p] * n_seq)

    def z_copy(src, b, p, d):
        return remote(src, raw.at[b, piece(p)], z_snd, z_rcv.at[b, p], mp=d)

    def relayed(b, d):
        return (((b == 1) & (d == 3)) | ((b == 2) & (d == 0))) & (RELAY == 1)

    def plane_copy(src, b, p):
        seq = jnp.where(b == c, mate, b * CORES + r)
        lane_in = jnp.where(b == c, 1, 0)
        return remote(src, xk.at[place(p, s)], k_snd, k_rcv.at[lane_in, p], seq=seq)

    def z_send(p):
        ups, downs = (range(n_mp - 1, 0, -1), range(n_mp - 1))
        if NEAR:
            ups, downs = (ups[::-1], downs[::-1])
        for side, order in ((1, ups), (-1, downs)):
            for d in order:

                @pl.when(((d > m) if side > 0 else (d < m)) & jnp.logical_not(relayed(m, d)))
                def _():
                    z_copy(tok_ref.at[piece(p)], m, p, d).start()

    def send_own(p):
        plane_copy(tok_ref.at[piece(p)], m, p).start()

        @pl.when(m == c)
        def _():
            xk[place(p, s), :] = tok_ref[piece(p), :]

    def pass_on(p, k):
        low = m < n_mp // 2
        take(p, k, 1, low)
        take(p, k, -1, True)
        take(p, k, 1, jnp.logical_not(low))

    def take(p, k, sign, when):
        b = m + sign * k

        @pl.when((b >= 0) & (b <= n_mp - 1) & when)
        def _():
            here = raw.at[b, piece(p)]
            z_copy(here, b, p, m).wait_recv()
            if k == 1 and RELAY:
                far = n_mp - 1 if sign < 0 else 0

                @pl.when(m == (n_mp - 2 if sign < 0 else 1))
                def _():
                    z_copy(here, b, p, far).start()

            plane_copy(here, b, p).start()

            @pl.when(b == c)
            def _():
                xk[place(p, s), :] = raw[b, piece(p), :]

    z_send(0)
    send_own(0)
    across = lax.broadcasted_iota(jnp.int32, (rows, rows), 0) == lax.broadcasted_iota(
        jnp.int32, (rows, rows), 1
    )
    wide = tok_ref[...].astype(jnp.float32)
    squares = jnp.sum(wide * wide, axis=1, keepdims=True)
    squares = jnp.sum(jnp.where(across, squares, 0.0), axis=0, keepdims=True)
    sq_own[...] = jnp.broadcast_to(squares, sq_own.shape)
    for o in range(1, n_mp):
        remote(sq_own, sq_all.at[o], q_snd, q_rcv, mp=(m + o) % n_mp).start()
    for p in range(1, LOOK):
        z_send(p)
    for p in range(1, OWN):
        send_own(p)

    w_out_copies = [
        remote(w_piece(hbm, 1 - r, chip), w_place(i, chip, r), w_snd, w_rcv, seq=mate)
        for chip in range(n_chip)
        for i, hbm in enumerate((wc_hbm, wg_hbm))
    ]
    for copy in w_out_copies:
        copy.start()
    for copy in small:
        copy.wait()
    wide_rows = width // LANES
    gain = jnp.concatenate([gain_ref[pl.ds(c * wide_rows + i, 1), :] for i in range(wide_rows)], axis=1)
    bias = bg_ref[pl.ds(q, 1), :]
    half_gate = rg_ref[pl.ds(q, 1), :] * 0.5
    rec_gate = rg_ref[pl.ds(q, 1), :]
    rec_cand = rc_ref[pl.ds(q, 1), :]

    def stage_a(p):
        if p + LOOK < PIECES:
            z_send(p + LOOK)
        if p + OWN < PIECES:
            send_own(p + OWN)
        for k in range(1, n_mp):
            pass_on(p, k)
            if (p, k) == FACTORS_AT:
                factors()

    def factors():
        total = sq_own[...]
        others = sq_all.at[pl.ds(1, n_mp - 1)]
        remote(others, others, q_snd, q_rcv, mp=m).wait_recv()
        for o in range(1, n_mp):
            total = total + sq_all[o]
        f_own[...] = lax.rsqrt(total / (width * n_mp) + 1e-05)
        for o in range(1, n_seq):
            copy = remote(f_own, f_all.at[s], g_snd, g_rcv, seq=(s + o) % n_seq)
            copy.start()
        f_all[pl.ds(s, 1)] = f_own[...][None]

    def spread_factors():
        others = f_all.at[pl.ds(1, n_seq - 1)]
        remote(others, others, g_snd, g_rcv, seq=s).wait_recv()
        for i in range(n_seq):
            row = f_all[i, 0:1, :]
            column = jnp.sum(jnp.where(across, row, 0.0), axis=1, keepdims=True)
            column = jnp.broadcast_to(column, (rows, LANES))
            for start, size in zip(STARTS, SIZES):
                f_col[start * n_seq + i * size : start * n_seq + (i + 1) * size, :] = column[start : start + size, :]

    def arrived(p, lane_in):
        of = xk.at[pl.ds(0, (n_chip - 1 + lane_in) * SIZES[p])]
        remote(of, of, k_snd, k_rcv.at[lane_in, p], seq=s).wait_recv()

    def stage_b(p):
        arrived(p, 0)
        for o in range(1, n_chip):
            there = ((c + n_chip - o) % n_chip) * CORES + r
            copy = remote(
                xk.at[place(p, there)], xk.at[place(p, there)], f_snd, k_rcv.at[1, p], seq=mate
            )
            copy.start()

    def stage_c(p):
        arrived(p, 1)

        tile = SIZES[p] * n_seq

        @pl.loop(0, tile // GROUP, unroll=UNROLL)
        def _(i):
            at = pl.ds(pl.multiple_of(i * GROUP, GROUP), GROUP)
            of = pl.ds(pl.multiple_of(STARTS[p] * n_seq + i * GROUP, GROUP), GROUP)
            xn[at, :] = (xk[of, :].astype(jnp.float32) * f_col[of, 0:1] * gain).astype(jnp.bfloat16)

        def product(chip):
            return jnp.dot(xn[:tile, :], wk[chip], preferred_element_type=jnp.float32)

        beside, above = near
        mid = tile // 2
        psend[1, block(p), :] = product(n_chip - 1 - c).astype(jnp.bfloat16)
        sums(1, p, 0, beside).start()
        sums(1, p, 1, above).start()
        value = product(beside)
        psend[0, split(p, 0), :] = value[:mid].astype(jnp.bfloat16)
        onward[split(p, 1), :] = value[mid:]
        sums(0, p, 0, beside).start()
        value = product(above)
        psend[0, split(p, 1), :] = value[mid:].astype(jnp.bfloat16)
        onward[split(p, 0), :] = value[:mid]
        sums(0, p, 1, above).start()
        own[block(p), :] = product(c)

    near = (c + 1 - 2 * (c % 2), (c + n_chip // 2) % n_chip)

    def split(p, h):
        mid = SIZES[p] * n_seq // 2
        return pl.ds(STARTS[p] * n_seq + h * mid, mid)

    def sums(slot, p, h, chip):
        at = split(p, h)
        return remote(
            psend.at[slot, at], precv.at[slot, at], p_snd, p_rcv.at[h if slot == 1 else 2, p], seq=chip * CORES + r
        )

    def stage_d(p):
        for h in range(2):
            sums(1, p, h, near[h]).wait_recv()
            mid = SIZES[p] * n_seq // 2

            @pl.loop(0, mid // GROUP)
            def _(i):
                at = pl.ds(pl.multiple_of(STARTS[p] * n_seq + h * mid + i * GROUP, GROUP), GROUP)
                psend[2, at, :] = (onward[at, :] + precv[1, at, :].astype(jnp.float32)).astype(jnp.bfloat16)

            sums(2, p, h, near[1 - h]).start()

    for turn in range(PIECES + CL + LAG):
        if turn == WO_TURN:
            wo_copy.start()
        for what in ORDER:
            if what == "a" and turn < PIECES:
                stage_a(turn)
            if what == "c" and 0 <= turn - CL < PIECES:
                if turn == CL:
                    spread_factors()
                    part = wk.at[pl.ds(0, n_chip // 2)]
                    pltpu.make_async_copy(part, part, w_loc).wait()
                    remote(part, part, w_snd, w_rcv, seq=s).wait_recv()
                stage_c(turn - CL)
            if what == "b" and 0 <= turn - BL < PIECES:
                stage_b(turn - BL)
            if what == "d" and 0 <= turn - CL - LAG < PIECES:
                stage_d(turn - CL - LAG)

    def gather_piece(p):
        both = precv.at[pl.ds(0, 2), block(p)]
        remote(both, both, p_snd, p_rcv.at[2, p], seq=s).wait_recv()

        @pl.loop(0, SIZES[p] * n_seq // GROUP)
        def _(i):
            at = pl.ds(pl.multiple_of(STARTS[p] * n_seq + i * GROUP, GROUP), GROUP)
            value = own[at, :]
            for slot in (0, 2):
                value = value + precv[slot, at, :].astype(jnp.float32)
            cand_n[at, :] = value[:, :LANES]
            gate_n[at, :] = (value[:, LANES:] + bias) * 0.5

    for newton_step in range(NEWTON):
        zero = jnp.zeros((n_seq, LANES), jnp.float32)
        entering = zero if newton_step == 0 else carry[...]
        held = (entering, zero + 1.0, zero)
        for p in range(PIECES):
            if newton_step == 0:
                gather_piece(p)

            def lap(i, held):
                previous, a, b = held
                j = STARTS[p] + i
                at = pl.ds(STARTS[p] * n_seq + i, n_seq, stride=SIZES[p])
                slope, offset = linear(newton_step == 0, previous, cand_n[at, :], gate_n[at, :], half_gate, rec_gate, rec_cand)
                if newton_step > 0:
                    previous = sweep_a[j] * entering + sweep_b[j]
                a, b = (slope * a, slope * b + offset)
                sweep_a[j] = a
                sweep_b[j] = b
                return (previous, a, b)

            held = lax.fori_loop(0, SIZES[p], lap, held, unroll=8)
        _, a, b = held
        state = jnp.zeros((1, LANES), jnp.float32)
        for i in range(n_seq):
            carry[i : i + 1, :] = state
            state = a[i : i + 1, :] * state + b[i : i + 1, :]
    entering = carry[...]
    for p in range(PIECES):

        @pl.loop(0, SIZES[p], unroll=8)
        def _(i):
            j = STARTS[p] + i
            cand_n[pl.ds(STARTS[p] * n_seq + i, n_seq, stride=SIZES[p]), :] = sweep_a[j] * entering + sweep_b[j]

    for i in range(n_seq):
        for p in range(PIECES):
            start, size = STARTS[p] * n_seq + i * SIZES[p], SIZES[p]
            ssend[i, piece(p), :] = cand_n[start : start + size, :].astype(jnp.bfloat16)
    lane = pl.ds(pl.multiple_of(q * LANES, LANES), LANES)
    for o in range(1, n_seq):
        there = (s + o) % n_seq
        copy = remote(ssend.at[there], sall.at[:, lane], s_snd, s_rcv, seq=there)
        copy.start()
    sall[:, lane] = ssend[pl.ds(s, 1)].reshape(rows, LANES)
    def sent(ref, sem):
        remote(ref, ref, sem, s_rcv, seq=s).wait_send()

    sent(wk.at[pl.ds(0, n_chip // 2)], w_snd)
    sent(raw.at[pl.ds(0, n_mp - 1)], z_snd)
    sent(raw, k_snd)
    sent(raw.at[pl.ds(0, n_chip - 1)], f_snd)
    sent(sq_all.at[pl.ds(1, n_mp - 1)], q_snd)
    sent(f_all.at[pl.ds(1, n_seq - 1)], g_snd)
    sent(psend, p_snd)
    wo_copy.wait()
    others = ssend.at[pl.ds(1, n_seq - 1)]
    remote(others, others, s_snd, s_rcv, seq=s).wait_recv()

    cols = out_ref.shape[1]
    half = rows // HALVES

    def hop(side, d, h):
        there = (m + 1) % n_mp if side == 0 else (m + n_mp - 1) % n_mp
        at = pl.ds(h * half, half)
        return remote(
            osend.at[d, at], orecv.at[side, d, at], o_snd, o_rcv.at[side, d, h], mp=there
        )

    def project(d):
        lanes = pl.ds(pl.multiple_of(d * cols, cols), cols)
        pout[...] = jnp.dot(sall[...], wo[:, lanes], preferred_element_type=jnp.float32)

    def send_sum(side, k, when):
        d = m + k if side == 0 else m - k
        inside = (d <= n_mp - 1) if side == 0 else (d >= 0)
        first = (m == 0) if side == 0 else (m == n_mp - 1)

        @pl.when(inside & when)
        def _():
            project(d)
            for h in range(HALVES):
                at = pl.ds(h * half, half)

                @pl.when(first)
                def _():
                    osend[d, at, :] = pout[at, :].astype(jnp.bfloat16)

                @pl.when(jnp.logical_not(first))
                def _():
                    hop(side, d, h).wait_recv()
                    osend[d, at, :] = (pout[at, :] + orecv[side, d, at, :].astype(jnp.float32)).astype(
                        jnp.bfloat16
                    )

                hop(side, d, h).start()

    for k in range(n_mp - 1, 1, -1):
        for side in range(2):
            send_sum(side, k, True)
    low = m < n_mp // 2
    send_sum(1, 1, low)
    send_sum(0, 1, True)
    send_sum(1, 1, jnp.logical_not(low))

    project(m)
    for side in range(2):

        @pl.when(m > 0 if side == 0 else m < n_mp - 1)
        def _():
            for h in range(HALVES):
                at = pl.ds(h * half, half)
                hop(side, m, h).wait_recv()
                pout[at, :] = pout[at, :] + orecv[side, m, at, :].astype(jnp.float32)

    out_ref[...] = pout[...].astype(jnp.bfloat16)

    sent(ssend.at[pl.ds(1, n_seq - 1)], s_snd)
    sent(osend.at[pl.ds(1, n_mp - 1)], o_snd)


def fused(n_seq, n_mp, tokens, norm_gain, w_cand, w_gate, rec_gate, rec_cand, bias_gate, w_out):
    rows, width = tokens.shape
    k_own, channels = w_cand.shape
    n_chip = n_seq // CORES
    length = rows * n_seq
    bf16, f32 = (jnp.bfloat16, jnp.float32)
    vmem, dma = (pltpu.VMEM, pltpu.SemaphoreType.DMA)
    whole = pl.BlockSpec(memory_space=pltpu.VMEM)
    far = pl.BlockSpec(memory_space=pl.ANY)
    per_channel = [part.reshape(n_seq, LANES) for part in (rec_gate, rec_cand, bias_gate)]
    return pl.pallas_call(
        functools.partial(fused_kernel, n_seq, n_mp),
        out_shape=pltpu.VMEM((rows, width), bf16),
        in_specs=[far] * 8,
        out_specs=whole,
        scratch_shapes=[
            vmem((rows, width), bf16),
            vmem((n_mp * width // LANES, LANES), f32),
            vmem((n_seq, LANES), f32),
            vmem((n_seq, LANES), f32),
            vmem((n_seq, LANES), f32),
            vmem((n_mp, rows, width), bf16),
            vmem((length, width), bf16),
            vmem((length * max(SIZES) // sum(SIZES), width), bf16),
            vmem((n_seq, LANES), f32),
            vmem((n_mp, n_seq, LANES), f32),
            vmem((n_seq, LANES), f32),
            vmem((n_seq, n_seq, LANES), f32),
            vmem((length, LANES), f32),
            vmem((n_chip, k_own * CORES, 2 * LANES), bf16),
            vmem(w_out.shape, bf16),
            vmem((length, 2 * LANES), f32),
            vmem((length, 2 * LANES), f32),
            vmem((n_chip - 1, length, 2 * LANES), bf16),
            vmem((n_chip - 1, length, 2 * LANES), bf16),
            vmem((length, LANES), f32),
            vmem((length, LANES), f32),
            vmem((rows, n_seq, LANES), f32),
            vmem((rows, n_seq, LANES), f32),
            vmem((n_seq, LANES), f32),
            vmem((n_seq, rows, LANES), bf16),
            vmem((rows, channels), bf16),
            vmem((rows, width), f32),
            vmem((n_mp, rows, width), bf16),
            vmem((2, n_mp, rows, width), bf16),
            dma,
            dma,
            dma,
            dma,
            dma,
            dma((4,)),
            dma,
            dma((n_mp, PIECES)),
            dma,
            dma((2, PIECES)),
            dma,
            dma,
            dma,
            dma,
            dma,
            dma,
            dma((3, PIECES)),
            dma,
            dma,
            dma,
            dma((2, n_mp, HALVES)),
        ],
        compiler_params=pltpu.CompilerParams(collective_id=0, has_side_effects=True),
    )(tokens, norm_gain.reshape(-1, LANES), w_cand, w_gate, *per_channel, w_out)


def layer(n_seq, n_mp, *args):
    tokens, w_cand = (args[0], args[2])
    fits = (
        n_seq == SUBLANES
        and n_seq == 4 * CORES
        and n_seq // CORES == n_mp
        and w_cand.shape[1] == n_seq * LANES
        and tokens.shape[0] == LANES
        and tokens.shape[1] % LANES == 0
    )
    return fused(n_seq, n_mp, *args) if fits else per_device(*args)


def solution(mesh):
    placed = (
        P("seq", "mp"),
        P(),
        P("seq", "mp"),
        P("seq", "mp"),
        P("mp"),
        P("mp"),
        P("mp"),
        P("mp", None),
    )
    return jax.shard_map(
        functools.partial(layer, mesh.shape["seq"], mesh.shape["mp"]), mesh=mesh, in_specs=placed, out_specs=P("seq", "mp"), check_vma=False
    )
```

```python
import functools

import jax
import jax.numpy as jnp
from jax import lax
from jax.experimental import pallas as pl
from jax.experimental.pallas import tpu as pltpu
from jax.sharding import PartitionSpec as P

NEWTON = 3


def prefix(value, axis, join, neutral):
    count, mine = (lax.axis_size(axis), lax.axis_index(axis))
    pieces = jax.tree.map(lambda part: lax.all_gather(part, axis), value)
    subtotal = jax.tree.map(
        lambda part, zero: jnp.full_like(part, 0) + jnp.asarray(zero, part.dtype), value, neutral
    )

    def lap(position, subtotal):
        longer = join(subtotal, jax.tree.map(lambda part: part[position], pieces))
        return jax.tree.map(lambda new, old: jnp.where(position < mine, new, old), longer, subtotal)

    return lax.fori_loop(0, count - 1, lap, subtotal)


def compose(earlier, later):
    return (later[0] * earlier[0], later[0] * earlier[1] + later[1])


def cell(previous, cand_pre, gate_pre, rec_gate, rec_cand, bias_gate):
    gate = jax.nn.sigmoid(gate_pre + rec_gate * previous + bias_gate)
    cand = jnp.tanh(cand_pre + rec_cand * previous)
    value = gate * previous + (1.0 - gate) * cand
    slope = (
        gate
        + gate * (1.0 - gate) * rec_gate * (previous - cand)
        + (1.0 - gate) * (1.0 - cand * cand) * rec_cand
    )
    return (value, slope)


def per_device(tokens, norm_gain, w_cand, w_gate, rec_gate, rec_cand, bias_gate, w_out):
    tok_rows = tokens.shape[0]
    channels = w_cand.shape[1]
    whole = lax.all_gather(tokens, "mp", axis=1, tiled=True)
    wide = whole.astype(jnp.float32)
    factor = lax.rsqrt(jnp.mean(wide * wide, axis=1, keepdims=True) + 1e-05)
    normed = (wide * factor * norm_gain).astype(jnp.bfloat16)
    cand_pre = jnp.dot(
        normed,
        lax.all_gather(w_cand, "seq", axis=0, tiled=True),
        preferred_element_type=jnp.float32,
    )
    gate_pre = jnp.dot(
        normed,
        lax.all_gather(w_gate, "seq", axis=0, tiled=True),
        preferred_element_type=jnp.float32,
    )
    state = jnp.zeros((tok_rows, channels), jnp.float32)
    carried = jnp.zeros((channels,), jnp.float32)
    ones_row = jnp.ones((channels,), jnp.float32)
    for newton_step in range(NEWTON):
        previous = jnp.concatenate([carried[None, :], state[:-1]], axis=0)
        value, slope = cell(previous, cand_pre, gate_pre, rec_gate, rec_cand, bias_gate)
        offset = value - slope * previous
        sweep_a, sweep_b = lax.associative_scan(compose, (slope, offset), axis=0)
        entering = prefix((sweep_a[-1], sweep_b[-1]), "seq", compose, (ones_row, carried * 0.0))
        carried = entering[1]
        state = sweep_a * carried + sweep_b
    state_b = state.astype(jnp.bfloat16)
    partial_sums = jnp.dot(state_b, w_out, preferred_element_type=jnp.float32)
    summed = lax.psum_scatter(partial_sums, "mp", scatter_dimension=1, tiled=True)
    return summed.astype(jnp.bfloat16)


def linear(first, previous, cand_pre, half_pre, half_gate, rec_gate, rec_cand):
    if first:
        gate = 0.5 * jnp.tanh(half_pre) + 0.5
        cand = jnp.tanh(cand_pre)
        apart = -cand
    else:
        gate = 0.5 * jnp.tanh(half_pre + half_gate * previous) + 0.5
        cand = jnp.tanh(cand_pre + rec_cand * previous)
        apart = previous - cand
    other = 1.0 - gate
    moved = gate * apart
    slope = gate + other * (rec_gate * moved + rec_cand * (1.0 - cand * cand))
    offset = cand + moved
    return slope, offset if first else offset - slope * previous


CORES = 2
SUBLANES = 8
LANES = 128
SIZES = (16, 16, 32, 32, 16, 16)
PIECES = len(SIZES)
STARTS = tuple(sum(SIZES[:i]) for i in range(PIECES))
HALVES = 2
RELAY = 1
NEAR = 1
FACTORS_AT = (0, 2)
LAG = 2
LOOK = 2
WO_TURN = 6
UNROLL = 4
OWN = 1
BL = 1
CL = 2
ORDER = "acbd"
GROUP = 16
MESH = pl.DeviceIdType.MESH


def fused_kernel(
    n_seq,
    n_mp,
    tok_hbm,
    gain_hbm,
    wc_hbm,
    wg_hbm,
    rg_hbm,
    rc_hbm,
    bg_hbm,
    wo_hbm,
    out_ref,
    tok_ref,
    gain_ref,
    rg_ref,
    rc_ref,
    bg_ref,
    raw,
    xk,
    xn,
    sq_own,
    sq_all,
    f_own,
    f_all,
    f_col,
    wk,
    wo,
    own,
    onward,
    psend,
    precv,
    cand_n,
    gate_n,
    sweep_a,
    sweep_b,
    carry,
    ssend,
    sall,
    pout,
    osend,
    orecv,
    w_loc,
    w_snd,
    w_rcv,
    wo_sem,
    tok_sem,
    small_sem,
    z_snd,
    z_rcv,
    k_snd,
    k_rcv,
    f_snd,
    q_snd,
    q_rcv,
    g_snd,
    g_rcv,
    p_snd,
    p_rcv,
    s_snd,
    s_rcv,
    o_snd,
    o_rcv,
):
    s, m = (lax.axis_index("seq"), lax.axis_index("mp"))
    n_chip = n_seq // CORES
    c, r = (s // CORES, s % CORES)
    mate = c * CORES + (1 - r)
    rows = tok_ref.shape[0]
    tokens = rows * n_seq
    k_own = wc_hbm.shape[0]
    width = raw.shape[2]
    q = r * n_chip + c

    def remote(src, dst, snd, rcv, **where):
        return pltpu.make_async_remote_copy(
            src_ref=src, dst_ref=dst, send_sem=snd, recv_sem=rcv, device_id=where, device_id_type=MESH
        )

    def greet():
        sem = pltpu.get_barrier_semaphore()
        for o in range(1, n_seq):
            pl.semaphore_signal(sem, inc=1, device_id={"seq": (s + o) % n_seq}, device_id_type=MESH)
        for o in range(1, n_mp):
            pl.semaphore_signal(sem, inc=1, device_id={"mp": (m + o) % n_mp}, device_id_type=MESH)

    def w_piece(hbm, core, chip):
        return hbm.at[:, pl.ds(pl.multiple_of((core * n_chip + chip) * LANES, LANES), LANES)]

    def w_place(i, chip, core):
        return wk.at[chip, pl.ds(pl.multiple_of(core * k_own, k_own), k_own), pl.ds(i * LANES, LANES)]

    local = [
        pltpu.make_async_copy(w_piece(hbm, r, chip), w_place(i, chip, r), w_loc)
        for chip in range(n_chip)
        for i, hbm in enumerate((wc_hbm, wg_hbm))
    ]
    wo_copy = pltpu.make_async_copy(wo_hbm, wo, wo_sem)
    greet()
    tok_copy = pltpu.make_async_copy(tok_hbm, tok_ref, tok_sem)
    tok_copy.start()
    for copy in local:
        copy.start()
    small = [
        pltpu.make_async_copy(src, dst, small_sem.at[i])
        for i, (src, dst) in enumerate(
            ((gain_hbm, gain_ref), (rg_hbm, rg_ref), (rc_hbm, rc_ref), (bg_hbm, bg_ref))
        )
    ]
    for copy in small:
        copy.start()
    pl.semaphore_wait(pltpu.get_barrier_semaphore(), n_seq + n_mp - 2)
    tok_copy.wait()

    def piece(p):
        return pl.ds(STARTS[p], SIZES[p])

    def place(p, seq):
        return pl.ds(pl.multiple_of(STARTS[p] * n_seq + seq * SIZES[p], SUBLANES * 2), SIZES[p])

    def block(p):
        return pl.ds(STARTS[p] * n_seq, SIZES[p] * n_seq)

    def z_copy(src, b, p, d):
        return remote(src, raw.at[b, piece(p)], z_snd, z_rcv.at[b, p], mp=d)

    def relayed(b, d):
        return (((b == 1) & (d == 3)) | ((b == 2) & (d == 0))) & (RELAY == 1)

    def plane_copy(src, b, p):
        seq = jnp.where(b == c, mate, b * CORES + r)
        lane_in = jnp.where(b == c, 1, 0)
        return remote(src, xk.at[place(p, s)], k_snd, k_rcv.at[lane_in, p], seq=seq)

    def z_send(p):
        ups, downs = (range(n_mp - 1, 0, -1), range(n_mp - 1))
        if NEAR:
            ups, downs = (ups[::-1], downs[::-1])
        for side, order in ((1, ups), (-1, downs)):
            for d in order:

                @pl.when(((d > m) if side > 0 else (d < m)) & jnp.logical_not(relayed(m, d)))
                def _():
                    z_copy(tok_ref.at[piece(p)], m, p, d).start()

    def send_own(p):
        plane_copy(tok_ref.at[piece(p)], m, p).start()

        @pl.when(m == c)
        def _():
            xk[place(p, s), :] = tok_ref[piece(p), :]

    def pass_on(p, k):
        low = m < n_mp // 2
        take(p, k, 1, low)
        take(p, k, -1, True)
        take(p, k, 1, jnp.logical_not(low))

    def take(p, k, sign, when):
        b = m + sign * k

        @pl.when((b >= 0) & (b <= n_mp - 1) & when)
        def _():
            here = raw.at[b, piece(p)]
            z_copy(here, b, p, m).wait_recv()
            if k == 1 and RELAY:
                far = n_mp - 1 if sign < 0 else 0

                @pl.when(m == (n_mp - 2 if sign < 0 else 1))
                def _():
                    z_copy(here, b, p, far).start()

            plane_copy(here, b, p).start()

            @pl.when(b == c)
            def _():
                xk[place(p, s), :] = raw[b, piece(p), :]

    z_send(0)
    send_own(0)
    across = lax.broadcasted_iota(jnp.int32, (rows, rows), 0) == lax.broadcasted_iota(
        jnp.int32, (rows, rows), 1
    )
    wide = tok_ref[...].astype(jnp.float32)
    squares = jnp.sum(wide * wide, axis=1, keepdims=True)
    squares = jnp.sum(jnp.where(across, squares, 0.0), axis=0, keepdims=True)
    sq_own[...] = jnp.broadcast_to(squares, sq_own.shape)
    for o in range(1, n_mp):
        remote(sq_own, sq_all.at[o], q_snd, q_rcv, mp=(m + o) % n_mp).start()
    for p in range(1, LOOK):
        z_send(p)
    for p in range(1, OWN):
        send_own(p)

    w_out_copies = [
        remote(w_piece(hbm, 1 - r, chip), w_place(i, chip, r), w_snd, w_rcv, seq=mate)
        for chip in range(n_chip)
        for i, hbm in enumerate((wc_hbm, wg_hbm))
    ]
    for copy in w_out_copies:
        copy.start()
    for copy in small:
        copy.wait()
    wide_rows = width // LANES
    gain = jnp.concatenate([gain_ref[pl.ds(c * wide_rows + i, 1), :] for i in range(wide_rows)], axis=1)
    bias = bg_ref[pl.ds(q, 1), :]
    half_gate = rg_ref[pl.ds(q, 1), :] * 0.5
    rec_gate = rg_ref[pl.ds(q, 1), :]
    rec_cand = rc_ref[pl.ds(q, 1), :]

    def stage_a(p):
        if p + LOOK < PIECES:
            z_send(p + LOOK)
        if p + OWN < PIECES:
            send_own(p + OWN)
        for k in range(1, n_mp):
            pass_on(p, k)
            if (p, k) == FACTORS_AT:
                factors()

    def factors():
        total = sq_own[...]
        others = sq_all.at[pl.ds(1, n_mp - 1)]
        remote(others, others, q_snd, q_rcv, mp=m).wait_recv()
        for o in range(1, n_mp):
            total = total + sq_all[o]
        f_own[...] = lax.rsqrt(total / (width * n_mp) + 1e-05)
        for o in range(1, n_seq):
            copy = remote(f_own, f_all.at[s], g_snd, g_rcv, seq=(s + o) % n_seq)
            copy.start()
        f_all[pl.ds(s, 1)] = f_own[...][None]

    def spread_factors():
        others = f_all.at[pl.ds(1, n_seq - 1)]
        remote(others, others, g_snd, g_rcv, seq=s).wait_recv()
        for i in range(n_seq):
            row = f_all[i, 0:1, :]
            column = jnp.sum(jnp.where(across, row, 0.0), axis=1, keepdims=True)
            column = jnp.broadcast_to(column, (rows, LANES))
            for start, size in zip(STARTS, SIZES):
                f_col[start * n_seq + i * size : start * n_seq + (i + 1) * size, :] = column[start : start + size, :]

    def arrived(p, lane_in):
        of = xk.at[pl.ds(0, (n_chip - 1 + lane_in) * SIZES[p])]
        remote(of, of, k_snd, k_rcv.at[lane_in, p], seq=s).wait_recv()

    def stage_b(p):
        arrived(p, 0)
        for o in range(1, n_chip):
            there = ((c + n_chip - o) % n_chip) * CORES + r
            copy = remote(
                xk.at[place(p, there)], xk.at[place(p, there)], f_snd, k_rcv.at[1, p], seq=mate
            )
            copy.start()

    def stage_c(p):
        arrived(p, 1)

        tile = SIZES[p] * n_seq

        @pl.loop(0, tile // GROUP, unroll=UNROLL)
        def _(i):
            at = pl.ds(pl.multiple_of(i * GROUP, GROUP), GROUP)
            of = pl.ds(pl.multiple_of(STARTS[p] * n_seq + i * GROUP, GROUP), GROUP)
            xn[at, :] = (xk[of, :].astype(jnp.float32) * f_col[of, 0:1] * gain).astype(jnp.bfloat16)

        def product(chip):
            return jnp.dot(xn[:tile, :], wk[chip], preferred_element_type=jnp.float32)

        beside, above = near
        mid = tile // 2
        psend[1, block(p), :] = product(n_chip - 1 - c).astype(jnp.bfloat16)
        sums(1, p, 0, beside).start()
        sums(1, p, 1, above).start()
        value = product(beside)
        psend[0, split(p, 0), :] = value[:mid].astype(jnp.bfloat16)
        onward[split(p, 1), :] = value[mid:]
        sums(0, p, 0, beside).start()
        value = product(above)
        psend[0, split(p, 1), :] = value[mid:].astype(jnp.bfloat16)
        onward[split(p, 0), :] = value[:mid]
        sums(0, p, 1, above).start()
        own[block(p), :] = product(c)

    near = (c + 1 - 2 * (c % 2), (c + n_chip // 2) % n_chip)

    def split(p, h):
        mid = SIZES[p] * n_seq // 2
        return pl.ds(STARTS[p] * n_seq + h * mid, mid)

    def sums(slot, p, h, chip):
        at = split(p, h)
        return remote(
            psend.at[slot, at], precv.at[slot, at], p_snd, p_rcv.at[h if slot == 1 else 2, p], seq=chip * CORES + r
        )

    def stage_d(p):
        for h in range(2):
            sums(1, p, h, near[h]).wait_recv()
            mid = SIZES[p] * n_seq // 2

            @pl.loop(0, mid // GROUP)
            def _(i):
                at = pl.ds(pl.multiple_of(STARTS[p] * n_seq + h * mid + i * GROUP, GROUP), GROUP)
                psend[2, at, :] = (onward[at, :] + precv[1, at, :].astype(jnp.float32)).astype(jnp.bfloat16)

            sums(2, p, h, near[1 - h]).start()

    for turn in range(PIECES + CL + LAG):
        if turn == WO_TURN:
            wo_copy.start()
        for what in ORDER:
            if what == "a" and turn < PIECES:
                stage_a(turn)
            if what == "c" and 0 <= turn - CL < PIECES:
                if turn == CL:
                    spread_factors()
                    part = wk.at[pl.ds(0, n_chip // 2)]
                    pltpu.make_async_copy(part, part, w_loc).wait()
                    remote(part, part, w_snd, w_rcv, seq=s).wait_recv()
                stage_c(turn - CL)
            if what == "b" and 0 <= turn - BL < PIECES:
                stage_b(turn - BL)
            if what == "d" and 0 <= turn - CL - LAG < PIECES:
                stage_d(turn - CL - LAG)

    def gather_piece(p):
        both = precv.at[pl.ds(0, 2), block(p)]
        remote(both, both, p_snd, p_rcv.at[2, p], seq=s).wait_recv()

        @pl.loop(0, SIZES[p] * n_seq // GROUP)
        def _(i):
            at = pl.ds(pl.multiple_of(STARTS[p] * n_seq + i * GROUP, GROUP), GROUP)
            value = own[at, :]
            for slot in (0, 2):
                value = value + precv[slot, at, :].astype(jnp.float32)
            cand_n[at, :] = value[:, :LANES]
            gate_n[at, :] = (value[:, LANES:] + bias) * 0.5

    for newton_step in range(NEWTON):
        zero = jnp.zeros((n_seq, LANES), jnp.float32)
        entering = zero if newton_step == 0 else carry[...]
        held = (entering, zero + 1.0, zero)
        for p in range(PIECES):
            if newton_step == 0:
                gather_piece(p)

            def lap(i, held):
                previous, a, b = held
                j = STARTS[p] + i
                at = pl.ds(STARTS[p] * n_seq + i, n_seq, stride=SIZES[p])
                slope, offset = linear(newton_step == 0, previous, cand_n[at, :], gate_n[at, :], half_gate, rec_gate, rec_cand)
                if newton_step > 0:
                    previous = sweep_a[j] * entering + sweep_b[j]
                a, b = (slope * a, slope * b + offset)
                sweep_a[j] = a
                sweep_b[j] = b
                return (previous, a, b)

            held = lax.fori_loop(0, SIZES[p], lap, held, unroll=8)
        _, a, b = held
        state = jnp.zeros((1, LANES), jnp.float32)
        for i in range(n_seq):
            carry[i : i + 1, :] = state
            state = a[i : i + 1, :] * state + b[i : i + 1, :]
    entering = carry[...]
    for p in range(PIECES):

        @pl.loop(0, SIZES[p], unroll=8)
        def _(i):
            j = STARTS[p] + i
            cand_n[pl.ds(STARTS[p] * n_seq + i, n_seq, stride=SIZES[p]), :] = sweep_a[j] * entering + sweep_b[j]

    def rounded(seq):
        for p in range(PIECES):
            ssend[pl.ds(seq, 1), piece(p), :] = cand_n[place(p, seq), :].astype(jnp.bfloat16)[None]

    lane = pl.ds(pl.multiple_of(q * LANES, LANES), LANES)
    for o in range(1, n_seq):
        there = (s + o) % n_seq
        rounded(there)
        copy = remote(ssend.at[there], sall.at[:, lane], s_snd, s_rcv, seq=there)
        copy.start()
    rounded(s)
    sall[:, lane] = ssend[pl.ds(s, 1)].reshape(rows, LANES)
    def sent(ref, sem):
        remote(ref, ref, sem, s_rcv, seq=s).wait_send()

    sent(wk.at[pl.ds(0, n_chip // 2)], w_snd)
    sent(raw.at[pl.ds(0, n_mp - 1)], z_snd)
    sent(raw, k_snd)
    sent(raw.at[pl.ds(0, n_chip - 1)], f_snd)
    sent(sq_all.at[pl.ds(1, n_mp - 1)], q_snd)
    sent(f_all.at[pl.ds(1, n_seq - 1)], g_snd)
    sent(psend, p_snd)
    wo_copy.wait()
    others = ssend.at[pl.ds(1, n_seq - 1)]
    remote(others, others, s_snd, s_rcv, seq=s).wait_recv()

    cols = out_ref.shape[1]
    half = rows // HALVES

    def hop(side, d, h):
        there = (m + 1) % n_mp if side == 0 else (m + n_mp - 1) % n_mp
        at = pl.ds(h * half, half)
        return remote(
            osend.at[d, at], orecv.at[side, d, at], o_snd, o_rcv.at[side, d, h], mp=there
        )

    def project(d):
        lanes = pl.ds(pl.multiple_of(d * cols, cols), cols)
        pout[...] = jnp.dot(sall[...], wo[:, lanes], preferred_element_type=jnp.float32)

    def send_sum(side, k, when):
        d = m + k if side == 0 else m - k
        inside = (d <= n_mp - 1) if side == 0 else (d >= 0)
        first = (m == 0) if side == 0 else (m == n_mp - 1)

        @pl.when(inside & when)
        def _():
            project(d)
            for h in range(HALVES):
                at = pl.ds(h * half, half)

                @pl.when(first)
                def _():
                    osend[d, at, :] = pout[at, :].astype(jnp.bfloat16)

                @pl.when(jnp.logical_not(first))
                def _():
                    hop(side, d, h).wait_recv()
                    osend[d, at, :] = (pout[at, :] + orecv[side, d, at, :].astype(jnp.float32)).astype(
                        jnp.bfloat16
                    )

                hop(side, d, h).start()

    for k in range(n_mp - 1, 1, -1):
        for side in range(2):
            send_sum(side, k, True)
    low = m < n_mp // 2
    send_sum(1, 1, low)
    send_sum(0, 1, True)
    send_sum(1, 1, jnp.logical_not(low))

    project(m)
    for side in range(2):

        @pl.when(m > 0 if side == 0 else m < n_mp - 1)
        def _():
            for h in range(HALVES):
                at = pl.ds(h * half, half)
                hop(side, m, h).wait_recv()
                pout[at, :] = pout[at, :] + orecv[side, m, at, :].astype(jnp.float32)

    out_ref[...] = pout[...].astype(jnp.bfloat16)

    sent(ssend.at[pl.ds(1, n_seq - 1)], s_snd)
    sent(osend.at[pl.ds(1, n_mp - 1)], o_snd)


def fused(n_seq, n_mp, tokens, norm_gain, w_cand, w_gate, rec_gate, rec_cand, bias_gate, w_out):
    rows, width = tokens.shape
    k_own, channels = w_cand.shape
    n_chip = n_seq // CORES
    length = rows * n_seq
    bf16, f32 = (jnp.bfloat16, jnp.float32)
    vmem, dma = (pltpu.VMEM, pltpu.SemaphoreType.DMA)
    whole = pl.BlockSpec(memory_space=pltpu.VMEM)
    far = pl.BlockSpec(memory_space=pl.ANY)
    per_channel = [part.reshape(n_seq, LANES) for part in (rec_gate, rec_cand, bias_gate)]
    return pl.pallas_call(
        functools.partial(fused_kernel, n_seq, n_mp),
        out_shape=pltpu.VMEM((rows, width), bf16),
        in_specs=[far] * 8,
        out_specs=whole,
        scratch_shapes=[
            vmem((rows, width), bf16),
            vmem((n_mp * width // LANES, LANES), f32),
            vmem((n_seq, LANES), f32),
            vmem((n_seq, LANES), f32),
            vmem((n_seq, LANES), f32),
            vmem((n_mp, rows, width), bf16),
            vmem((length, width), bf16),
            vmem((length * max(SIZES) // sum(SIZES), width), bf16),
            vmem((n_seq, LANES), f32),
            vmem((n_mp, n_seq, LANES), f32),
            vmem((n_seq, LANES), f32),
            vmem((n_seq, n_seq, LANES), f32),
            vmem((length, LANES), f32),
            vmem((n_chip, k_own * CORES, 2 * LANES), bf16),
            vmem(w_out.shape, bf16),
            vmem((length, 2 * LANES), f32),
            vmem((length, 2 * LANES), f32),
            vmem((n_chip - 1, length, 2 * LANES), bf16),
            vmem((n_chip - 1, length, 2 * LANES), bf16),
            vmem((length, LANES), f32),
            vmem((length, LANES), f32),
            vmem((rows, n_seq, LANES), f32),
            vmem((rows, n_seq, LANES), f32),
            vmem((n_seq, LANES), f32),
            vmem((n_seq, rows, LANES), bf16),
            vmem((rows, channels), bf16),
            vmem((rows, width), f32),
            vmem((n_mp, rows, width), bf16),
            vmem((2, n_mp, rows, width), bf16),
            dma,
            dma,
            dma,
            dma,
            dma,
            dma((4,)),
            dma,
            dma((n_mp, PIECES)),
            dma,
            dma((2, PIECES)),
            dma,
            dma,
            dma,
            dma,
            dma,
            dma,
            dma((3, PIECES)),
            dma,
            dma,
            dma,
            dma((2, n_mp, HALVES)),
        ],
        compiler_params=pltpu.CompilerParams(collective_id=0, has_side_effects=True),
    )(tokens, norm_gain.reshape(-1, LANES), w_cand, w_gate, *per_channel, w_out)


def layer(n_seq, n_mp, *args):
    tokens, w_cand = (args[0], args[2])
    fits = (
        n_seq == SUBLANES
        and n_seq == 4 * CORES
        and n_seq // CORES == n_mp
        and w_cand.shape[1] == n_seq * LANES
        and tokens.shape[0] == LANES
        and tokens.shape[1] % LANES == 0
    )
    return fused(n_seq, n_mp, *args) if fits else per_device(*args)


def solution(mesh):
    placed = (
        P("seq", "mp"),
        P(),
        P("seq", "mp"),
        P("seq", "mp"),
        P("mp"),
        P("mp"),
        P("mp"),
        P("mp", None),
    )
    return jax.shard_map(
        functools.partial(layer, mesh.shape["seq"], mesh.shape["mp"]), mesh=mesh, in_specs=placed, out_specs=P("seq", "mp"), check_vma=False
    )
```
